256 devices in a mesh: wafer: 4 (over y), span: 64 (over z, x, core).
Axes of the slice: x: 4, y: 4, z: 8, core: 2. Of those that a mesh axis runs over, the one named last changes fastest.
Arguments:
- timestream: float32 [1536, 16384], P(('wafer', 'span')), may hold values from -6 to 6
- templates: float32 [64, 16384], P(None, 'span'), may hold values from -0.046875 to 0.046875
- bias_group: int32 [1536], P('wafer'), may hold values from 0 to 11, as said below
- det_weight: float32 [1536], P('wafer'), may hold values from 0.2 to 5
- cut_start: int32 [1536], P('wafer'), may hold values from 0 to 16383
- cut_len: int32 [1536], P('wafer'), may hold values from 1 to 511
- pointing: int32 [1536, 16384], P('wafer', 'span'), may hold values from 0 to 32767
- hit_tiles: int32 [64, 64], replicated, may hold values from 0 to 511, as said below
Outputs:
- fit_coeffs: float32 [1536, 64], P(('wafer', 'span'))
- rhs_map: float32 [512, 512], P('span', 'wafer')
- weight_map: float32 [512, 512], P('span', 'wafer')
The draws below stay inside these ranges and needn't reach their ends.
Inputs may be any that keep to these rules, and one draw needn't show every extreme that they name: `bias_group`: within each wafer's 384 detectors every bias line holds exactly 32 detectors. `hit_tiles`: each row lists distinct tiles; tile t is owned by index t // 8 of span; every row holds exactly 2 tiles of each owner it names: of one owner common to all rows, and of 31 other owners.
All inputs are finite; a program needn't handle non-finite values.
Results may differ from the reference program's by a relative error of at most 0.0041.
Values sent between devices are 32-bit elements; how exact they have to be, the bound alone decides.
No kernel may reach another device: no remote copies, remote signals or barrier semaphores. Data moves between devices by JAX's collectives and lax.ppermute only.
A program may use at most 64 MiB of HBM per device.

```python
import math
import jax
import jax.numpy as jnp
from jax import lax

TCH = 256
NT = 64
NGROUP = 12
TILE = 512
TILE_OWN = 8
CAP = 2
DET_W = 384
DET = 1536
SAMP = 16384
HIT = 64
NTILE = 512


def draw_bias_group(key, part):
    wafers = DET // DET_W

    def one_wafer(wafer_index):
        order = jax.random.permutation(jax.random.fold_in(key, wafer_index), DET_W)
        return (order % NGROUP).astype(jnp.int32)
    return jax.vmap(one_wafer)(jnp.arange(wafers, dtype=jnp.int32)).reshape(DET)


def draw_hit_tiles(key, part):
    owner_count = NTILE // TILE_OWN
    other_count = HIT // CAP - 1
    center = jax.random.randint(jax.random.fold_in(key, 7), (), 0, owner_count)

    def one_span(span_index):
        span_key = jax.random.fold_in(key, 1000 + span_index)
        scores = jax.random.randint(jax.random.fold_in(span_key, 1), (owner_count - 1,), 0, 2 ** 30)
        others = jnp.argsort(scores, stable=True)[:other_count].astype(jnp.int32)
        others = others + (others >= center).astype(jnp.int32)
        tile_scores = jax.random.randint(jax.random.fold_in(span_key, 2), (other_count, TILE_OWN), 0, 2 ** 30)
        within = jnp.argsort(tile_scores, axis=1, stable=True)[:, :CAP].astype(jnp.int32)
        central = center * TILE_OWN + TILE_OWN - CAP + jnp.arange(CAP, dtype=jnp.int32)
        spread = (others[:, None] * TILE_OWN + within).reshape(-1)
        listed = jnp.concatenate([central, spread])
        order = jax.random.permutation(jax.random.fold_in(span_key, 3), HIT)
        return listed[order].astype(jnp.int32)
    return jax.vmap(one_span)(jnp.arange(owner_count, dtype=jnp.int32))


def with_ends(values, rng, smallest, high):
    shape = values.shape
    spot = [jax.random.randint(jax.random.fold_in(rng, axis), (), 0, shape[axis]) for axis in range(len(shape))]
    values = values.at[tuple(spot)].set(smallest)
    longest = shape.index(max(shape))
    spot[longest] = (spot[longest] + 1) % shape[longest]
    return values.at[tuple(spot)].set(high)


def levels(own_key, shape, shards, smallest, high):
    factor_of, own = 1.0, jax.random.fold_in(own_key, 6)
    for dim, parts in shards:
        steps = jnp.exp(jax.random.uniform(jax.random.fold_in(own, dim), (parts,), jnp.float32, smallest / len(shards), high / len(shards)))
        factor_of = factor_of * jnp.repeat(steps, shape[dim] // parts).reshape([-1 if axis == dim else 1 for axis in range(len(shape))])
    return factor_of


def noise(key, shape, scale, most, pieces=(), held_as=jnp.bfloat16):
    factor_of = levels(key, shape, pieces, -0.22, 0.18) if pieces else 1.0
    drawn = jax.random.normal(key, shape, jnp.float32) * scale * factor_of
    return jnp.minimum(jnp.maximum(drawn, -most), most).astype(held_as)


def setup_inputs(seed: int = 0) -> dict:
    arg_keys = jax.random.split(jax.random.key(seed), 9)
    timestream = noise(arg_keys[0], (DET, SAMP), 1.0, 6.0, ((0, 256),), jnp.float32)
    templates = noise(arg_keys[1], (NT, SAMP), SAMP ** -0.5, 0.046875, ((1, 64),), jnp.float32)
    bias_group = draw_bias_group(jax.random.fold_in(arg_keys[8], 71), 0)
    det_weight = jnp.clip(jnp.exp(math.log(5.0) - 3.218876 * jax.random.uniform(arg_keys[3], (DET,), jnp.float32) ** levels(arg_keys[3], (DET,), ((0, 4),), -0.2, 0.2)), 0.2, 5.0)
    cut_start = with_ends(jax.random.randint(arg_keys[4], (DET,), 0, SAMP), jax.random.fold_in(arg_keys[4], 1), 0, SAMP - 1).astype(jnp.int32)
    cut_len = with_ends(jax.random.randint(arg_keys[5], (DET,), 1, 2 * TCH), jax.random.fold_in(arg_keys[5], 1), 1, (2 * TCH) - 1).astype(jnp.int32)
    pointing = with_ends(jax.random.randint(arg_keys[6], (DET, SAMP), 0, HIT * TILE), jax.random.fold_in(arg_keys[6], 1), 0, (HIT * TILE) - 1).astype(jnp.int32)
    hit_tiles = draw_hit_tiles(jax.random.fold_in(arg_keys[8], 71), 0)
    return {"timestream": timestream, "templates": templates, "bias_group": bias_group, "det_weight": det_weight, "cut_start": cut_start, "cut_len": cut_len, "pointing": pointing, "hit_tiles": hit_tiles}


def solve_normal(matrix, right_side):
    factor = jnp.linalg.cholesky(matrix)
    middle = lax.linalg.triangular_solve(factor, right_side, left_side=True, lower=True)
    return lax.linalg.triangular_solve(factor, middle, left_side=True, lower=True, transpose_a=True)

def reference(timestream, templates, bias_group, det_weight, cut_start, cut_len, pointing, hit_tiles):
    highest = lax.Precision.HIGHEST
    wafers = DET // DET_W
    by_wafer = timestream.reshape(wafers, DET_W, SAMP)
    wafer_groups = bias_group.reshape(wafers, DET_W)
    onehot = (wafer_groups[:, None, :] == jnp.arange(NGROUP, dtype=jnp.int32)[None, :, None]).astype(jnp.float32)
    line_mean = jnp.einsum('wgd,wds->wgs', onehot, by_wafer, precision=highest) * (NGROUP / DET_W)
    common = jnp.einsum('wgd,wgs->wds', onehot, line_mean, precision=highest)
    cleaned = (by_wafer - common).reshape(DET, SAMP)
    gram = jnp.dot(templates.astype(jnp.float32), templates.T.astype(jnp.float32), precision=highest, preferred_element_type=jnp.float32)
    projection = jnp.dot(templates.astype(jnp.float32), cleaned.T.astype(jnp.float32), precision=highest, preferred_element_type=jnp.float32)
    amplitudes = solve_normal(gram, projection)
    filtered = cleaned - jnp.dot(amplitudes.T.astype(jnp.float32), templates.astype(jnp.float32), precision=highest, preferred_element_type=jnp.float32)
    sample_time = jnp.arange(SAMP, dtype=jnp.int32)
    inside = (sample_time[None, :] >= cut_start[:, None]) & (sample_time[None, :] < (cut_start + cut_len)[:, None])
    sample_weight = jnp.where(inside, jnp.float32(0.0), det_weight[:, None]).astype(jnp.bfloat16)
    weighted = (sample_weight.astype(jnp.float32) * filtered).astype(jnp.bfloat16)
    span_of = sample_time // TCH
    tile_index = hit_tiles[span_of[None, :], pointing // TILE]
    pixel = (tile_index * TILE + pointing % TILE).astype(jnp.int32).reshape(-1)
    rhs_map = jax.ops.segment_sum(weighted.astype(jnp.float32).reshape(-1), pixel, num_segments=NTILE * TILE)
    weight_map = jax.ops.segment_sum(sample_weight.astype(jnp.float32).reshape(-1), pixel, num_segments=NTILE * TILE)
    return (amplitudes.T, rhs_map.reshape(NTILE, TILE), weight_map.reshape(NTILE, TILE))
```

```python
import jax
import jax.numpy as jnp
from jax import lax
from jax.experimental import pallas as pl
from jax.experimental.pallas import tpu as pltpu
from jax.sharding import PartitionSpec as P

NGROUP = 12
TILE = 512
TILE_OWN = 8
SPANS = 64
WAFERS = 4
DEV_DETS = 6
PAD_DETS = 8
WAFER_DETS = SPANS * DEV_DETS
SPAN_LEN = 256
NT = 64
HIT = 64
LANES = 128
CHUNK = 4
STEP_SPANS = 2

f32 = jnp.float32
bf16 = jnp.bfloat16
HIGHEST = lax.Precision.HIGHEST
VMEM = pl.BlockSpec(memory_space=pltpu.VMEM)
SMEM = pl.BlockSpec(memory_space=pltpu.SMEM)


def call(kernel, out_shape, name, in_specs, scratch_shapes=(), flops=0):
    return pl.pallas_call(
        kernel,
        out_shape=out_shape,
        in_specs=in_specs,
        out_specs=jax.tree.map(lambda unused: VMEM, out_shape),
        scratch_shapes=scratch_shapes,
        name=name,
        cost_estimate=pl.CostEstimate(flops=flops, bytes_accessed=1 << 20, transcendentals=0),
    )


def split3(value):
    high = value.astype(bf16)
    rest = value - high.astype(f32)
    middle = rest.astype(bf16)
    low = (rest - middle.astype(f32)).astype(bf16)
    return high, middle, low


def exact_left_dot(left, right):
    return sum(jnp.dot(left, piece, preferred_element_type=f32) for piece in split3(right))


def pack_kernel(stream_ref, templates_ref, out_ref):
    templates = templates_ref[...]
    gram = lax.dot_general(
        templates, templates, (((1,), (1,)), ((), ())), precision=HIGHEST, preferred_element_type=f32
    )
    out_ref[:, DEV_DETS:, :] = jnp.zeros((SPANS, PAD_DETS - DEV_DETS, SPAN_LEN), f32)
    for s in range(SPANS):
        out_ref[s, 0:DEV_DETS, :] = stream_ref[:, s * SPAN_LEN : (s + 1) * SPAN_LEN]
        out_ref[s, DEV_DETS : DEV_DETS + 1, 0:NT] = gram[s : s + 1, :]


def mixer_kernel(column_ref, row_ref, out_ref):
    rows = lax.broadcasted_iota(jnp.int32, (512, 512), 0)
    columns = lax.broadcasted_iota(jnp.int32, (512, 512), 1)
    same_line = (column_ref[...] == row_ref[...]) & (row_ref[...] >= 0)
    scale = NGROUP / WAFER_DETS
    keep = jnp.where((rows == columns) & (row_ref[...] >= 0), 1.0, 0.0)
    out_ref[...] = (keep - jnp.where(same_line, scale, 0.0)).astype(bf16)


def project_kernel(received_ref, mixer_ref, templates_ref, cleaned_ref, out_ref, scratch):
    received = received_ref[...]
    scratch[...] = received[:, :LANES]
    gram_row = jnp.sum(scratch[pl.ds(DEV_DETS, SPANS, stride=PAD_DETS), :], axis=0, keepdims=True)
    cleaned = exact_left_dot(mixer_ref[...], received)
    cleaned_ref[...] = cleaned
    templates = templates_ref[...]
    twice = jnp.concatenate([templates, templates], axis=0)
    scratch[...] = lax.dot_general(
        cleaned, twice, (((1,), (1,)), ((), ())), precision=HIGHEST, preferred_element_type=f32
    )
    first_half = lax.broadcasted_iota(jnp.int32, (SPANS, LANES), 1) < NT
    for r in range(3):
        out_ref[pl.ds(r, SPANS, stride=CHUNK), :] = jnp.where(
            first_half,
            scratch[pl.ds(r, SPANS, stride=PAD_DETS), :],
            scratch[pl.ds(r + 3, SPANS, stride=PAD_DETS), :],
        )
    out_ref[pl.ds(3, SPANS, stride=CHUNK), :] = jnp.broadcast_to(gram_row, (SPANS, LANES))


def total_kernel(received_ref, out_ref):
    total = received_ref[0:8, :]
    for k in range(1, 32):
        total = total + received_ref[8 * k : 8 * k + 8, :]
    total = total + pltpu.roll(total, 4, 0)
    for k in range(32):
        out_ref[8 * k : 8 * k + 8, :] = total


def factor_kernel(received_ref, out_ref):
    gram = received_ref[pl.ds(3, SPANS, stride=CHUNK), :]
    lane = lax.broadcasted_iota(jnp.int32, (NT, LANES), 1)
    row = lax.broadcasted_iota(jnp.int32, (NT, LANES), 0)
    work = jnp.where(lane < NT, gram, jnp.where(lane - NT == row, 1.0, 0.0))
    pivots = jnp.zeros((NT, 1), f32)
    row_index = row[:, :1]
    for k in range(NT):
        pivot = work[k : k + 1, k : k + 1]
        ratio = jnp.where(row_index > k, work[:, k : k + 1] / pivot, 0.0)
        pivots = jnp.where(row_index == k, pivot, pivots)
        work = work - ratio * work[k : k + 1, :]
    inverse = work * lax.rsqrt(pivots)
    lower = jnp.where(lane < NT, pltpu.roll(inverse, NT, 1), 0.0)
    upper = jnp.where(lane < NT, 0.0, inverse)
    out_ref[0:NT, :] = lower
    out_ref[NT:, :] = upper


def bin_kernel(
    base_ref, gathered_ref, inverse_ref, templates_ref, cleaned_ref, pointing_ref, weight_ref, start_ref,
    stop_ref, coeffs_ref, out_ref, fitted_low, fitted_high, totals
):
    inverse = inverse_ref[...]
    middle = lax.dot_general(
        gathered_ref[...], inverse, (((1,), (1,)), ((), ())), precision=HIGHEST, preferred_element_type=f32
    )
    coeffs = jnp.dot(middle, inverse, precision=HIGHEST, preferred_element_type=f32)
    coeffs_ref[...] = coeffs
    templates = templates_ref[...]
    blank = jnp.zeros_like(templates)
    fitted_low[...] = jnp.dot(
        coeffs, jnp.concatenate([templates, blank], axis=0), precision=HIGHEST, preferred_element_type=f32
    )
    fitted_high[...] = jnp.dot(
        coeffs, jnp.concatenate([blank, templates], axis=0), precision=HIGHEST, preferred_element_type=f32
    )
    totals[...] = jnp.zeros_like(totals)
    out_ref[...] = jnp.zeros_like(out_ref)
    labels = lax.broadcasted_iota(jnp.int32, (256, SPAN_LEN), 0).astype(f32).astype(bf16)
    time = lax.broadcasted_iota(jnp.int32, (PAD_DETS, SPAN_LEN), 1)
    zero = jnp.zeros((16, SPAN_LEN), bf16)
    one = jnp.ones((16, SPAN_LEN), bf16)

    def spread(row):
        return jnp.broadcast_to(row, (16, SPAN_LEN)).astype(bf16)

    def step(n, carry):
        first = pl.multiple_of(n * (STEP_SPANS * CHUNK), STEP_SPANS * CHUNK)
        low = fitted_low[pl.ds(first, STEP_SPANS * CHUNK), :]
        high = fitted_high[pl.ds(first, STEP_SPANS * CHUNK), :]
        left, right = [], []
        for k in range(STEP_SPANS):
            s = n * STEP_SPANS + k
            clean = cleaned_ref[pl.ds(pl.multiple_of(s * PAD_DETS, PAD_DETS), PAD_DETS), :]
            inside = (time >= start_ref[s]) & (time < stop_ref[s])
            weight = jnp.where(inside, 0.0, weight_ref[s]).astype(bf16).astype(f32)
            for i in range(DEV_DETS):
                fitted = (low if i < 3 else high)[CHUNK * k + i % 3 : CHUNK * k + i % 3 + 1, :]
                weight_row = weight[i : i + 1, :]
                value = weight_row * (clean[i : i + 1, :] - fitted)
                point = pointing_ref[pl.ds(s * DEV_DETS + i, 1), :]
                coarse = spread((point >> 8).astype(f32))
                fine = spread((point & 255).astype(f32))
                value, weight_row = spread(value), spread(weight_row)
                hits = [labels[16 * m : 16 * m + 16] == coarse for m in range(8)]
                left.append(
                    jnp.concatenate(
                        [jnp.where(hit, value, zero) for hit in hits]
                        + [jnp.where(hit, weight_row, zero) for hit in hits],
                        axis=0,
                    )
                )
                right.append(
                    jnp.concatenate(
                        [jnp.where(labels[16 * m : 16 * m + 16] == fine, one, zero) for m in range(16)], axis=0
                    )
                )
        totals[...] += lax.dot_general(
            jnp.concatenate(left, axis=1),
            jnp.concatenate(right, axis=1),
            (((1,), (1,)), ((), ())),
            preferred_element_type=f32,
        )
        return carry

    lax.fori_loop(0, SPANS // STEP_SPANS, step, 0)

    def place(j, carry):
        base = base_ref[j]
        for kind in range(2):
            for quarter in range(4):
                row = totals[pl.ds(kind * 128 + j * 2 + quarter // 2, 1), :]
                lanes = slice((quarter % 2) * LANES, (quarter % 2 + 1) * LANES)
                out_ref[pl.ds(quarter * (SPANS * CHUNK) + base + kind * 2, 1), :] = row[:, lanes]
        return carry

    lax.fori_loop(0, HIT, place, 0)


def merge_kernel(received_ref, tile_ref, rhs_ref, weight_ref):
    rows = SPANS * CHUNK
    total = received_ref[0:rows, :]
    for w in range(1, WAFERS):
        total = total + received_ref[w * rows : (w + 1) * rows, :]
    wanted = lax.broadcasted_iota(jnp.int32, (16, rows), 0)
    column = lax.broadcasted_iota(jnp.int32, (16, rows), 1)
    chosen = (tile_ref[...] == wanted % 8) & ((column % CHUNK) // 2 == wanted // 8)
    selector = jnp.where(chosen, 1.0, 0.0).astype(bf16)
    merged = exact_left_dot(selector, total)
    rhs_ref[...] = merged[0:8, :]
    weight_ref[...] = merged[8:16, :]


def shape(*dims, dtype=f32):
    return jax.ShapeDtypeStruct(dims, dtype)


def padded(values, fill):
    return jnp.pad(values.reshape(SPANS, DEV_DETS), ((0, 0), (0, PAD_DETS - DEV_DETS)), constant_values=fill)


def body(timestream, templates, bias_group, det_weight, cut_start, cut_len, pointing, hit_tiles):
    own = lax.axis_index("span")
    outgoing = call(pack_kernel, shape(SPANS, PAD_DETS, SPAN_LEN), "pack", [VMEM, VMEM])(timestream, templates)
    received = lax.all_to_all(outgoing, "span", split_axis=0, concat_axis=0, tiled=True)

    groups = padded(bias_group, -1).reshape(512)
    mixer = call(mixer_kernel, shape(512, 512, dtype=bf16), "mixer", [VMEM, VMEM])(groups[:, None], groups[None, :])
    span_start = own * SPAN_LEN
    starts = padded(cut_start - span_start, 0)[:, :, None]
    stops = padded(cut_start + cut_len - span_start, 0)[:, :, None]
    weights = padded(det_weight, 0)[:, :, None]
    own_owner = lax.dynamic_index_in_dim(hit_tiles, own, 0, keepdims=False) // TILE_OWN
    order = jnp.arange(HIT, dtype=jnp.int32)
    earlier = (own_owner[None, :] == own_owner[:, None]) & (order[None, :] < order[:, None])
    base = own_owner * CHUNK + jnp.sum(earlier.astype(jnp.int32), axis=1)
    mine = hit_tiles // TILE_OWN == own
    position = jnp.broadcast_to(order[None, :], (SPANS, HIT))
    first = jnp.min(jnp.where(mine, position, HIT), axis=1, keepdims=True)
    last = jnp.max(jnp.where(mine, position, -1), axis=1, keepdims=True)
    within = hit_tiles % TILE_OWN + 1
    first_tile = jnp.sum(jnp.where(position == first, within, 0), axis=1) - 1
    last_tile = jnp.sum(jnp.where(position == last, within, 0), axis=1) - 1
    slot_tile = jnp.stack([first_tile, last_tile, first_tile, last_tile], axis=1).reshape(1, SPANS * CHUNK)

    cleaned, partial = call(
        project_kernel, (shape(512, SPAN_LEN), shape(SPANS * CHUNK, LANES)), "project", [VMEM] * 3,
        [pltpu.VMEM((512, LANES), f32)],
    )(received.reshape(512, SPAN_LEN), mixer, templates)
    partial = lax.all_to_all(
        partial.reshape(SPANS, CHUNK, LANES), "span", split_axis=0, concat_axis=0, tiled=True
    ).reshape(SPANS * CHUNK, LANES)
    totals = call(total_kernel, shape(SPANS * CHUNK, LANES), "total", [VMEM])(partial)
    gathered = lax.all_to_all(
        totals.reshape(SPANS, CHUNK, LANES), "span", split_axis=0, concat_axis=0, tiled=True
    ).reshape(SPANS * CHUNK, LANES)
    inverse = call(factor_kernel, shape(LANES, LANES), "factor", [VMEM])(partial)
    coeffs, tiles = call(
        bin_kernel, (shape(SPANS * CHUNK, LANES), shape(WAFERS * SPANS * CHUNK, LANES)), "bin",
        [SMEM] + [VMEM] * 8,
        [pltpu.VMEM((SPANS * CHUNK, SPAN_LEN), f32)] * 2 + [pltpu.VMEM((256, 256), f32)],
    )(base, gathered, inverse, templates, cleaned, pointing, weights, starts, stops)
    tiles = lax.all_to_all(
        tiles.reshape(WAFERS * SPANS, CHUNK, LANES), ("wafer", "span"), split_axis=0, concat_axis=0, tiled=True
    ).reshape(WAFERS * SPANS * CHUNK, LANES)
    own_coeffs = lax.dynamic_slice_in_dim(coeffs, own * CHUNK, 3)
    fit_coeffs = jnp.concatenate([own_coeffs[:, :NT], own_coeffs[:, NT:]], axis=0)
    rhs_map, weight_map = call(merge_kernel, (shape(8, LANES), shape(8, LANES)), "merge", [VMEM, VMEM])(tiles, slot_tile)
    return (fit_coeffs, rhs_map, weight_map)


def solution(mesh):
    in_specs = (
        P(("wafer", "span"), None),
        P(None, "span"),
        P("wafer"),
        P("wafer"),
        P("wafer"),
        P("wafer"),
        P("wafer", "span"),
        P(),
    )
    out_specs = (P(("wafer", "span"), None), P("span", "wafer"), P("span", "wafer"))
    return jax.shard_map(body, mesh=mesh, in_specs=in_specs, out_specs=out_specs, check_vma=False)
```

```python
import jax
import jax.numpy as jnp
from jax import lax
from jax.experimental import pallas as pl
from jax.experimental.pallas import tpu as pltpu
from jax.sharding import PartitionSpec as P

NGROUP = 12
TILE = 512
TILE_OWN = 8
SPANS = 64
WAFERS = 4
DEV_DETS = 6
PAD_DETS = 8
WAFER_DETS = SPANS * DEV_DETS
SPAN_LEN = 256
NT = 64
HIT = 64
LANES = 128
CHUNK = 4
GROUPS = 4
FIRST_GROUPS = 2
GROUP_TIMES = SPAN_LEN // GROUPS

f32 = jnp.float32
bf16 = jnp.bfloat16
HIGHEST = lax.Precision.HIGHEST
VMEM = pl.BlockSpec(memory_space=pltpu.VMEM)
ANY = pl.BlockSpec(memory_space=pl.ANY)


def call(kernel, out_shape, name, in_specs, scratch_shapes=(), vmem=16):
    return pl.pallas_call(
        kernel,
        out_shape=out_shape,
        in_specs=in_specs,
        out_specs=jax.tree.map(lambda unused: VMEM, out_shape),
        scratch_shapes=scratch_shapes,
        name=name,
        compiler_params=pltpu.CompilerParams(vmem_limit_bytes=vmem << 20),
        cost_estimate=pl.CostEstimate(flops=1 << 30, bytes_accessed=1 << 20, transcendentals=0),
    )


def split3(value):
    high = value.astype(bf16)
    rest = value - high.astype(f32)
    middle = rest.astype(bf16)
    low = (rest - middle.astype(f32)).astype(bf16)
    return high, middle, low


def exact_left_dot(left, right):
    return sum(jnp.dot(left, piece, preferred_element_type=f32) for piece in split3(right))


def pack_kernel(stream_ref, templates_ref, out_ref):
    templates = templates_ref[...]
    gram = lax.dot_general(
        templates, templates, (((1,), (1,)), ((), ())), precision=HIGHEST, preferred_element_type=f32
    )
    out_ref[:, DEV_DETS:, :] = jnp.zeros((SPANS, PAD_DETS - DEV_DETS, SPAN_LEN), f32)
    for s in range(SPANS):
        out_ref[s, 0:DEV_DETS, :] = stream_ref[:, s * SPAN_LEN : (s + 1) * SPAN_LEN]
        out_ref[s, DEV_DETS : DEV_DETS + 1, 0:NT] = gram[s : s + 1, :]


def total_kernel(received_ref, after_ref, out_ref):
    total = received_ref[0:8, :]
    for k in range(1, 32):
        total = total + received_ref[8 * k : 8 * k + 8, :]
    total = total + pltpu.roll(total, 4, 0)
    for k in range(32):
        out_ref[8 * k : 8 * k + 8, :] = total


def factor_kernel(received_ref, out_ref):
    gram = received_ref[pl.ds(3, SPANS, stride=CHUNK), :]
    lane = lax.broadcasted_iota(jnp.int32, (NT, LANES), 1)
    row = lax.broadcasted_iota(jnp.int32, (NT, LANES), 0)
    work = jnp.where(lane < NT, gram, jnp.where(lane - NT == row, 1.0, 0.0))
    pivots = jnp.zeros((NT, 1), f32)
    row_index = row[:, :1]
    for k in range(NT):
        pivot = work[k : k + 1, k : k + 1]
        ratio = jnp.where(row_index > k, work[:, k : k + 1] / pivot, 0.0)
        pivots = jnp.where(row_index == k, pivot, pivots)
        work = work - ratio * work[k : k + 1, :]
    inverse = work * lax.rsqrt(pivots)
    lower = jnp.where(lane < NT, pltpu.roll(inverse, NT, 1), 0.0)
    upper = jnp.where(lane < NT, 0.0, inverse)
    out_ref[0:NT, :] = lower
    out_ref[NT:, :] = upper


def prepare_kernel(
    pointing_ref, column4_ref, column8_ref, row8_ref, row_ref, weight_ref, start_ref, stop_ref, after_ref,
    mixer4_ref, mixer_ref, coarse_ref, fine_ref, sample_weight_ref
):
    scale = NGROUP / WAFER_DETS

    def mix(out_shape, row_det, row_valid, column_det, column_valid, row_group, column_group):
        keep = jnp.where(row_det == column_det, 1.0, 0.0) - jnp.where(row_group == column_group, scale, 0.0)
        return jnp.where(row_valid & column_valid, keep, 0.0).astype(bf16)

    row = lax.broadcasted_iota(jnp.int32, (512, 512), 0)
    column = lax.broadcasted_iota(jnp.int32, (512, 512), 1)
    det4 = ((row >> 2) & (SPANS - 1)) * DEV_DETS + (row >> 8) * 3 + (row & 3)
    det8 = (column >> 3) * DEV_DETS + (column & 7)
    mixer4_ref[...] = mix(
        (512, 512), det4, (row & 3) < 3, det8, (column & 7) < DEV_DETS, column4_ref[...], row8_ref[...]
    )
    row = lax.broadcasted_iota(jnp.int32, (512, WAFER_DETS), 0)
    column = lax.broadcasted_iota(jnp.int32, (512, WAFER_DETS), 1)
    det8 = (row >> 3) * DEV_DETS + (row & 7)
    mixer_ref[...] = mix(
        (512, WAFER_DETS), det8, (row & 7) < DEV_DETS, column, column >= 0, column8_ref[...], row_ref[...]
    )
    pointing = pointing_ref[...]
    coarse_ref[...] = (pointing >> 8).astype(f32).T
    fine = (pointing & 255).astype(f32)
    for g in range(GROUPS):
        fine_ref[g] = fine[:, g * GROUP_TIMES : (g + 1) * GROUP_TIMES]
    time = lax.broadcasted_iota(jnp.int32, (SPAN_LEN, WAFER_DETS), 0)
    inside = (time >= start_ref[...]) & (time < stop_ref[...])
    weight = jnp.broadcast_to(weight_ref[...], (SPAN_LEN, WAFER_DETS))
    sample_weight_ref[...] = jnp.where(inside, 0.0, weight).astype(bf16).astype(f32)


def project_kernel(received_ref, mixer4_ref, templates_ref, after_ref, out_ref, scratch):
    received = received_ref[...]
    scratch[...] = received[:, :LANES]
    gram_row = jnp.sum(scratch[pl.ds(DEV_DETS, SPANS, stride=PAD_DETS), :], axis=0, keepdims=True)
    templates = templates_ref[...]
    twice = jnp.concatenate([templates, templates], axis=0)
    raw = lax.dot_general(
        received, twice, (((1,), (1,)), ((), ())), precision=HIGHEST, preferred_element_type=f32
    )
    mixed = exact_left_dot(mixer4_ref[...], raw)
    row = lax.broadcasted_iota(jnp.int32, (SPANS * CHUNK, LANES), 0)
    lane = lax.broadcasted_iota(jnp.int32, (SPANS * CHUNK, LANES), 1)
    halves = jnp.where(lane < NT, mixed[: SPANS * CHUNK], mixed[SPANS * CHUNK :])
    out_ref[...] = jnp.where((row & 3) == 3, jnp.broadcast_to(gram_row, halves.shape), halves)


def clean_kernel(received_ref, mixer_ref, after_ref, out_ref):
    mixer = mixer_ref[...]
    out_ref[...] = sum(
        lax.dot_general(piece, mixer, (((0,), (0,)), ((), ())), preferred_element_type=f32)
        for piece in split3(received_ref[...])
    )


def accumulate(values_ref, coarse_ref, fine_ref, totals_ref, first, last):
    labels = lax.broadcasted_iota(jnp.int32, (LANES, WAFER_DETS), 0).astype(f32).astype(bf16)
    lane = lax.broadcasted_iota(jnp.int32, (WAFER_DETS, LANES), 1)
    low_lane, high_lane = lane.astype(f32).astype(bf16), (lane + LANES).astype(f32).astype(bf16)
    one, zero = jnp.ones((WAFER_DETS, LANES), bf16), jnp.zeros((WAFER_DETS, LANES), bf16)
    blank = jnp.zeros((16, WAFER_DETS), bf16)

    def spread(rows, i):
        return jnp.broadcast_to(rows[i : i + 1], (16, WAFER_DETS)).astype(bf16)

    def step(g, carry):
        fine = fine_ref[g]
        left, right = [], []
        for block in range(GROUP_TIMES // 8):
            times = pl.ds(pl.multiple_of(g * GROUP_TIMES + 8 * block, 8), 8)
            coarse_rows, value_rows = coarse_ref[times, :], values_ref[times, :]
            for i in range(8):
                coarse, value = spread(coarse_rows, i), spread(value_rows, i)
                left.append(
                    jnp.concatenate(
                        [jnp.where(labels[16 * m : 16 * m + 16] == coarse, value, blank) for m in range(8)], axis=0
                    )
                )
                t = 8 * block + i
                point = jnp.broadcast_to(fine[:, t : t + 1], (WAFER_DETS, LANES)).astype(bf16)
                right.append(
                    jnp.concatenate(
                        [jnp.where(low_lane == point, one, zero), jnp.where(high_lane == point, one, zero)], axis=1
                    )
                )
        totals_ref[...] += jnp.dot(
            jnp.concatenate(left, axis=1), jnp.concatenate(right, axis=0), preferred_element_type=f32
        )
        return carry

    lax.fori_loop(first, last, step, 0)


def weight_first_kernel(sample_weight_ref, coarse_ref, fine_ref, out_ref):
    out_ref[...] = jnp.zeros_like(out_ref)
    accumulate(sample_weight_ref, coarse_ref, fine_ref, out_ref, 0, FIRST_GROUPS)


def weight_rest_kernel(sample_weight_ref, coarse_ref, fine_ref, totals_ref, after_ref, out_ref):
    out_ref[...] = totals_ref[...]
    accumulate(sample_weight_ref, coarse_ref, fine_ref, out_ref, FIRST_GROUPS, GROUPS)


def bin_kernel(
    gathered_ref, inverse_ref, templates_ref, cleaned_ref, sample_weight_ref, coarse_ref, fine_ref, weight_totals_ref,
    coeffs_ref, out_ref, values, totals, halves
):
    inverse = inverse_ref[...]
    middle = lax.dot_general(
        gathered_ref[...], inverse, (((1,), (1,)), ((), ())), precision=HIGHEST, preferred_element_type=f32
    )
    coeffs = jnp.dot(middle, inverse, precision=HIGHEST, preferred_element_type=f32)
    coeffs_ref[...] = coeffs
    det = lax.broadcasted_iota(jnp.int32, (WAFER_DETS, SPANS * CHUNK), 0)
    source = lax.broadcasted_iota(jnp.int32, (WAFER_DETS, SPANS * CHUNK), 1)
    place = det - DEV_DETS * (source >> 2) - (source & 3)
    selector = jnp.where(((place == 0) | (place == 3)) & ((source & 3) < 3), 1.0, 0.0).astype(bf16)
    both = exact_left_dot(selector, coeffs)
    part = lax.broadcasted_iota(jnp.int32, (WAFER_DETS, NT), 0) % DEV_DETS
    ordered = jnp.where(part < 3, both[:, :NT], both[:, NT:])
    fitted = lax.dot_general(
        templates_ref[...], ordered, (((0,), (1,)), ((), ())), precision=HIGHEST, preferred_element_type=f32
    )
    values[...] = sample_weight_ref[...] * (cleaned_ref[...] - fitted)
    totals[...] = jnp.zeros_like(totals)
    accumulate(values, coarse_ref, fine_ref, totals, 0, GROUPS)
    for kind, source_ref in enumerate((totals, weight_totals_ref)):
        for column in range(2):
            halves[...] = source_ref[:, column * LANES : (column + 1) * LANES]
            for half in range(2):
                out_ref[half * 2 + column, kind * HIT : (kind + 1) * HIT, :] = halves[pl.ds(half, HIT, stride=2), :]


def route_kernel(received_ref, slot_ref, out_ref):
    total = received_ref[0]
    for w in range(1, WAFERS):
        total = total + received_ref[w]
    row = lax.broadcasted_iota(jnp.int32, (SPANS * CHUNK, 2 * HIT), 0)
    selector = jnp.where(row == slot_ref[...], 1.0, 0.0).astype(bf16)
    out_ref[...] = exact_left_dot(selector, total)


def merge_kernel(received_ref, tile_ref, rhs_ref, weight_ref):
    rows = SPANS * CHUNK
    wanted = lax.broadcasted_iota(jnp.int32, (16, rows), 0)
    column = lax.broadcasted_iota(jnp.int32, (16, rows), 1)
    chosen = (tile_ref[...] == wanted % 8) & ((column % CHUNK) // 2 == wanted // 8)
    selector = jnp.where(chosen, 1.0, 0.0).astype(bf16)
    merged = exact_left_dot(selector, received_ref[...])
    rhs_ref[...] = merged[0:8, :]
    weight_ref[...] = merged[8:16, :]


def shape(*dims, dtype=f32):
    return jax.ShapeDtypeStruct(dims, dtype)


def exchange(values, axes, *dims):
    return lax.all_to_all(values.reshape(dims), axes, split_axis=0, concat_axis=0, tiled=True)


def body(timestream, templates, bias_group, det_weight, cut_start, cut_len, pointing, hit_tiles):
    own = lax.axis_index("span")
    outgoing = call(pack_kernel, shape(SPANS, PAD_DETS, SPAN_LEN), "pack", [VMEM, VMEM], vmem=60)(timestream, templates)
    received = exchange(outgoing, "span", SPANS, PAD_DETS, SPAN_LEN).reshape(512, SPAN_LEN)

    by_device = bias_group.reshape(SPANS, DEV_DETS)
    groups8 = jnp.pad(by_device, ((0, 0), (0, 2))).reshape(512)
    groups4 = jnp.pad(by_device.reshape(SPANS, 2, 3), ((0, 0), (0, 0), (0, 1))).transpose(1, 0, 2).reshape(512)
    start = cut_start - own * SPAN_LEN
    stop = start + cut_len
    mixer4, mixer, coarse, fine, sample_weight = call(
        prepare_kernel,
        (
            shape(512, 512, dtype=bf16), shape(512, WAFER_DETS, dtype=bf16), shape(SPAN_LEN, WAFER_DETS),
            shape(GROUPS, WAFER_DETS, GROUP_TIMES), shape(SPAN_LEN, WAFER_DETS),
        ),
        "prepare", [VMEM] * 8 + [ANY],
    )(
        pointing, groups4[:, None], groups8[:, None], groups8[None, :], bias_group[None, :], det_weight[None, :],
        start[None, :], stop[None, :], outgoing,
    )
    weight_totals = call(weight_first_kernel, shape(LANES, 2 * LANES), "weight_first", [VMEM] * 3, vmem=24)(
        sample_weight, coarse, fine
    )
    order = jnp.arange(HIT, dtype=jnp.int32)
    own_owner = lax.dynamic_index_in_dim(hit_tiles, own, 0, keepdims=False) // TILE_OWN
    earlier = (own_owner[None, :] == own_owner[:, None]) & (order[None, :] < order[:, None])
    base = own_owner * CHUNK + jnp.sum(earlier.astype(jnp.int32), axis=1)
    slot = jnp.concatenate([base, base + 2])[None, :]
    mine = hit_tiles // TILE_OWN == own
    position = jnp.broadcast_to(order[None, :], (SPANS, HIT))
    first = jnp.min(jnp.where(mine, position, HIT), axis=1, keepdims=True)
    last = jnp.max(jnp.where(mine, position, -1), axis=1, keepdims=True)
    within = hit_tiles % TILE_OWN + 1
    first_tile = jnp.sum(jnp.where(position == first, within, 0), axis=1) - 1
    last_tile = jnp.sum(jnp.where(position == last, within, 0), axis=1) - 1
    slot_tile = jnp.stack([first_tile, last_tile, first_tile, last_tile], axis=1).reshape(1, SPANS * CHUNK)

    partial = call(
        project_kernel, shape(SPANS * CHUNK, LANES), "project", [VMEM] * 3 + [ANY], [pltpu.VMEM((512, LANES), f32)]
    )(received, mixer4, templates, weight_totals)
    reduced = exchange(partial, "span", SPANS, CHUNK, LANES).reshape(SPANS * CHUNK, LANES)
    cleaned = call(clean_kernel, shape(SPAN_LEN, WAFER_DETS), "clean", [VMEM] * 2 + [ANY])(received, mixer, partial)
    weight_totals = call(weight_rest_kernel, shape(LANES, 2 * LANES), "weight_rest", [VMEM] * 4 + [ANY], vmem=24)(
        sample_weight, coarse, fine, weight_totals, cleaned
    )
    totals = call(total_kernel, shape(SPANS * CHUNK, LANES), "total", [VMEM, ANY])(reduced, weight_totals)
    gathered = exchange(totals, "span", SPANS, CHUNK, LANES).reshape(SPANS * CHUNK, LANES)
    inverse = call(factor_kernel, shape(LANES, LANES), "factor", [VMEM])(reduced)
    coeffs, tiles = call(
        bin_kernel, (shape(SPANS * CHUNK, LANES), shape(WAFERS, 2 * HIT, LANES)), "bin", [VMEM] * 8,
        [
            pltpu.VMEM((SPAN_LEN, WAFER_DETS), f32), pltpu.VMEM((LANES, 2 * LANES), f32),
            pltpu.VMEM((LANES, LANES), f32),
        ],
        vmem=24,
    )(gathered, inverse, templates, cleaned, sample_weight, coarse, fine, weight_totals)
    tiles = exchange(tiles, "wafer", WAFERS, 2 * HIT, LANES)
    routed = call(route_kernel, shape(SPANS * CHUNK, LANES), "route", [VMEM, VMEM])(tiles, slot)
    routed = exchange(routed, "span", SPANS, CHUNK, LANES).reshape(SPANS * CHUNK, LANES)
    own_coeffs = lax.dynamic_slice_in_dim(coeffs, own * CHUNK, 3)
    fit_coeffs = jnp.concatenate([own_coeffs[:, :NT], own_coeffs[:, NT:]], axis=0)
    rhs_map, weight_map = call(merge_kernel, (shape(8, LANES), shape(8, LANES)), "merge", [VMEM, VMEM])(
        routed, slot_tile
    )
    return (fit_coeffs, rhs_map, weight_map)


def solution(mesh):
    in_specs = (
        P(("wafer", "span"), None),
        P(None, "span"),
        P("wafer"),
        P("wafer"),
        P("wafer"),
        P("wafer"),
        P("wafer", "span"),
        P(),
    )
    out_specs = (P(("wafer", "span"), None), P("span", "wafer"), P("span", "wafer"))
    return jax.shard_map(body, mesh=mesh, in_specs=in_specs, out_specs=out_specs, check_vma=False)
```

```python
import jax
import jax.numpy as jnp
from jax import lax
from jax.experimental import pallas as pl
from jax.experimental.pallas import tpu as pltpu
from jax.sharding import PartitionSpec as P

NGROUP = 12
TILE = 512
TILE_OWN = 8
SPANS = 64
WAFERS = 4
PLANE = 8
DEPTH = SPANS // PLANE
DEV_DETS = 6
SENT = 2 * DEV_DETS + 1
WAFER_DETS = SPANS * DEV_DETS
SPAN_LEN = 256
NT = 64
HIT = 64
LANES = 128
CHUNK = 4
GROUPS = 4
FIRST_GROUPS = 3
GROUP_TIMES = SPAN_LEN // GROUPS

f32 = jnp.float32
bf16 = jnp.bfloat16
HIGHEST = lax.Precision.HIGHEST
VMEM = pl.BlockSpec(memory_space=pltpu.VMEM)
SMEM = pl.BlockSpec(memory_space=pltpu.SMEM)
ANY = pl.BlockSpec(memory_space=pl.ANY)


def call(kernel, out_shape, name, in_specs, scratch_shapes=(), vmem=16):
    return pl.pallas_call(
        kernel,
        out_shape=out_shape,
        in_specs=in_specs,
        out_specs=jax.tree.map(lambda unused: VMEM, out_shape),
        scratch_shapes=scratch_shapes,
        name=name,
        compiler_params=pltpu.CompilerParams(vmem_limit_bytes=vmem << 20),
        cost_estimate=pl.CostEstimate(flops=1 << 30, bytes_accessed=1 << 20, transcendentals=0),
    )


def split3(value):
    high = value.astype(bf16)
    rest = value - high.astype(f32)
    middle = rest.astype(bf16)
    low = (rest - middle.astype(f32)).astype(bf16)
    return high, middle, low


def exact_left_dot(left, right):
    return sum(jnp.dot(left, piece, preferred_element_type=f32) for piece in split3(right))


def pack_kernel(stream_ref, templates_ref, out_ref):
    templates = templates_ref[...]
    gram = lax.dot_general(
        templates, jnp.concatenate([templates, jnp.zeros_like(templates)], axis=0), (((1,), (1,)), ((), ())),
        precision=HIGHEST, preferred_element_type=f32,
    )
    for s in range(SPANS):
        for half in range(2):
            first = s * SPAN_LEN + half * LANES
            out_ref[pl.ds(s * SENT + half, DEV_DETS, stride=2), :] = stream_ref[:, first : first + LANES]
    out_ref[pl.ds(2 * DEV_DETS, SPANS, stride=SENT), :] = gram


def received_rows(received_ref):
    def rows(i, half):
        return jnp.concatenate(
            [received_ref[pl.ds(p * SENT + 2 * i + half, DEPTH, stride=PLANE * SENT), :] for p in range(PLANE)], axis=0
        )

    return jnp.concatenate(
        [jnp.concatenate([rows(i, 0), rows(i, 1)], axis=1) for i in range(DEV_DETS)], axis=0
    )


def lines(group_row):
    line = lax.broadcasted_iota(jnp.int32, (16, WAFER_DETS), 0)
    return jnp.where(line == group_row, 1.0, 0.0).astype(bf16)


def plane_total_kernel(received_ref, after_ref, out_ref):
    rows = DEPTH * CHUNK
    total = received_ref[0:rows, :]
    for k in range(1, PLANE):
        total = total + received_ref[rows * k : rows * (k + 1), :]
    gram_rows = received_ref[pl.ds(3, PLANE, stride=rows), :]
    for k in range(DEPTH):
        out_ref[rows * k : rows * (k + 1), :] = total
        out_ref[pl.ds(rows * k + 3, PLANE, stride=CHUNK), :] = gram_rows


def depth_total_kernel(received_ref, after_ref, out_ref):
    rows = DEPTH * CHUNK
    total = received_ref[0:rows, :]
    for k in range(1, DEPTH):
        total = total + received_ref[rows * k : rows * (k + 1), :]
    for k in range(PLANE):
        out_ref[rows * k : rows * (k + 1), :] = total


def factor_kernel(received_ref, out_ref):
    gram = received_ref[pl.ds(3, SPANS, stride=CHUNK), :]
    lane = lax.broadcasted_iota(jnp.int32, (NT, LANES), 1)
    row = lax.broadcasted_iota(jnp.int32, (NT, LANES), 0)
    work = jnp.where(lane < NT, gram, jnp.where(lane - NT == row, 1.0, 0.0))
    blocks = [work[8 * b : 8 * b + 8, :] for b in range(NT // 8)]
    sublane = lax.broadcasted_iota(jnp.int32, (8, LANES), 0)

    def lane_spread(block, k):
        return jnp.broadcast_to(block[:, k : k + 1], (8, LANES))

    for b in range(NT // 8):
        first = 8 * b
        rows = [jnp.broadcast_to(blocks[b][i : i + 1, :], (8, LANES)) for i in range(8)]
        corner = {(i, j): lane_spread(rows[i], first + j) for i in range(8) for j in range(i, 8)}
        columns = [[lane_spread(block, first + j) for block in blocks[b:]] for j in range(8)]
        for i in range(8):
            inverse = 1.0 / corner[i, i]
            ratios = [column * inverse for column in columns[i]]
            ratios[0] = jnp.where(sublane > i, ratios[0], 0.0)
            blocks[b:] = [block - ratio * rows[i] for block, ratio in zip(blocks[b:], ratios)]
            for j in range(i + 1, 8):
                shift = corner[i, j] * inverse
                rows[j] = rows[j] - shift * rows[i]
                columns[j] = [later - earlier * shift for later, earlier in zip(columns[j], columns[i])]
                for k in range(j, 8):
                    corner[j, k] = corner[j, k] - shift * corner[i, k]
    work = jnp.concatenate(blocks, axis=0)
    pivots = jnp.sum(jnp.where(lane == row, work, 0.0), axis=1, keepdims=True)
    inverse = work * lax.rsqrt(pivots)
    lower = jnp.where(lane < NT, pltpu.roll(inverse, NT, 1), 0.0)
    upper = jnp.where(lane < NT, 0.0, inverse)
    out_ref[0:NT, :] = lower
    out_ref[NT:, :] = upper


def prepare_kernel(
    own_ref, pointing_ref, weight_hbm, start_hbm, length_hbm, after_ref, coarse_ref, fine_ref, sample_weight_ref,
    weight_ref, start_ref, length_ref, semaphores
):
    copies = [
        pltpu.make_async_copy(source, target, semaphores.at[k])
        for k, (source, target) in enumerate(
            ((weight_hbm, weight_ref), (start_hbm, start_ref), (length_hbm, length_ref))
        )
    ]
    for copy in copies:
        copy.start()
    pointing = pointing_ref[...]
    coarse_ref[...] = (pointing >> 8).astype(f32).T
    fine = (pointing & 255).astype(f32)
    for g in range(GROUPS):
        fine_ref[g] = fine[:, g * GROUP_TIMES : (g + 1) * GROUP_TIMES]
    time = lax.broadcasted_iota(jnp.int32, (SPAN_LEN, WAFER_DETS), 0) + own_ref[0] * SPAN_LEN
    for copy in copies:
        copy.wait()
    start = start_ref[...].reshape(1, WAFER_DETS)
    stop = start + length_ref[...].reshape(1, WAFER_DETS)
    inside = (time >= start) & (time < stop)
    weight = jnp.broadcast_to(weight_ref[...].reshape(1, WAFER_DETS), (SPAN_LEN, WAFER_DETS))
    sample_weight_ref[...] = jnp.where(inside, 0.0, weight).astype(bf16).astype(f32)


def project_kernel(received_ref, group_ref, templates_ref, after_ref, out_ref):
    templates = templates_ref[...]
    raw = lax.dot_general(
        received_rows(received_ref), jnp.concatenate([templates, templates], axis=0), (((1,), (1,)), ((), ())),
        precision=HIGHEST, preferred_element_type=f32,
    )
    onehot = lines(group_ref[...])
    means = exact_left_dot(onehot, raw) * (NGROUP / WAFER_DETS)
    mixed = raw - sum(
        lax.dot_general(onehot, piece, (((0,), (0,)), ((), ())), preferred_element_type=f32) for piece in split3(means)
    )
    first_half = lax.broadcasted_iota(jnp.int32, (SPANS, LANES), 1) < NT
    for r in range(3):
        out_ref[pl.ds(r, SPANS, stride=CHUNK), :] = jnp.where(
            first_half, mixed[r * SPANS : (r + 1) * SPANS], mixed[(r + 3) * SPANS : (r + 4) * SPANS]
        )
    gram_row = jnp.sum(received_ref[pl.ds(2 * DEV_DETS, SPANS, stride=SENT), :], axis=0, keepdims=True)
    out_ref[pl.ds(3, SPANS, stride=CHUNK), :] = jnp.broadcast_to(gram_row, (SPANS, LANES))


def clean_kernel(received_ref, column_ref, row_ref, after_ref, out_ref):
    row = lax.broadcasted_iota(jnp.int32, (WAFER_DETS, WAFER_DETS), 0)
    column = lax.broadcasted_iota(jnp.int32, (WAFER_DETS, WAFER_DETS), 1)
    det = ((row % DEPTH) * PLANE + (row % SPANS) // DEPTH) * DEV_DETS + row // SPANS
    keep = jnp.where(det == column, 1.0, 0.0)
    mixer = (keep - jnp.where(column_ref[...] == row_ref[...], NGROUP / WAFER_DETS, 0.0)).astype(bf16)
    out_ref[...] = sum(
        lax.dot_general(piece, mixer, (((0,), (0,)), ((), ())), preferred_element_type=f32)
        for piece in split3(received_rows(received_ref))
    )


def accumulate(values_ref, coarse_ref, fine_ref, totals_ref, first, last):
    labels = lax.broadcasted_iota(jnp.int32, (LANES, WAFER_DETS), 0).astype(f32).astype(bf16)
    lane = lax.broadcasted_iota(jnp.int32, (WAFER_DETS, LANES), 1)
    low_lane, high_lane = lane.astype(f32).astype(bf16), (lane + LANES).astype(f32).astype(bf16)
    one, zero = jnp.ones((WAFER_DETS, LANES), bf16), jnp.zeros((WAFER_DETS, LANES), bf16)
    blank = jnp.zeros((16, WAFER_DETS), bf16)

    def spread(rows, i):
        return jnp.broadcast_to(rows[i : i + 1], (16, WAFER_DETS)).astype(bf16)

    def step(g, carry):
        fine = fine_ref[g]
        left, right = [], []
        for block in range(GROUP_TIMES // 8):
            times = pl.ds(pl.multiple_of(g * GROUP_TIMES + 8 * block, 8), 8)
            coarse_rows, value_rows = coarse_ref[times, :], values_ref[times, :]
            for i in range(8):
                coarse, value = spread(coarse_rows, i), spread(value_rows, i)
                left.append(
                    jnp.concatenate(
                        [jnp.where(labels[16 * m : 16 * m + 16] == coarse, value, blank) for m in range(8)], axis=0
                    )
                )
                t = 8 * block + i
                point = jnp.broadcast_to(fine[:, t : t + 1], (WAFER_DETS, LANES)).astype(bf16)
                right.append(
                    jnp.concatenate(
                        [jnp.where(low_lane == point, one, zero), jnp.where(high_lane == point, one, zero)], axis=1
                    )
                )
        totals_ref[...] += jnp.dot(
            jnp.concatenate(left, axis=1), jnp.concatenate(right, axis=0), preferred_element_type=f32
        )
        return carry

    lax.fori_loop(first, last, step, 0)


def weight_first_kernel(sample_weight_ref, coarse_ref, fine_ref, out_ref):
    out_ref[...] = jnp.zeros_like(out_ref)
    accumulate(sample_weight_ref, coarse_ref, fine_ref, out_ref, 0, FIRST_GROUPS)


def weight_rest_kernel(sample_weight_ref, coarse_ref, fine_ref, totals_ref, after_ref, out_ref):
    out_ref[...] = totals_ref[...]
    accumulate(sample_weight_ref, coarse_ref, fine_ref, out_ref, FIRST_GROUPS, GROUPS)


def bin_kernel(
    gathered_ref, inverse_ref, templates_ref, cleaned_ref, sample_weight_ref, coarse_ref, fine_ref, weight_totals_ref,
    coeffs_ref, out_ref, values, totals, halves
):
    inverse = inverse_ref[...]
    middle = lax.dot_general(
        gathered_ref[...], inverse, (((1,), (1,)), ((), ())), precision=HIGHEST, preferred_element_type=f32
    )
    coeffs = jnp.dot(middle, inverse, precision=HIGHEST, preferred_element_type=f32)
    coeffs_ref[...] = coeffs
    det = lax.broadcasted_iota(jnp.int32, (WAFER_DETS, SPANS * CHUNK), 0)
    source = lax.broadcasted_iota(jnp.int32, (WAFER_DETS, SPANS * CHUNK), 1)
    span = ((source >> 2) % DEPTH) * PLANE + (source >> 2) // DEPTH
    place = det - DEV_DETS * span - (source & 3)
    selector = jnp.where(((place == 0) | (place == 3)) & ((source & 3) < 3), 1.0, 0.0).astype(bf16)
    both = exact_left_dot(selector, coeffs)
    part = lax.broadcasted_iota(jnp.int32, (WAFER_DETS, NT), 0) % DEV_DETS
    ordered = jnp.where(part < 3, both[:, :NT], both[:, NT:])
    fitted = lax.dot_general(
        templates_ref[...], ordered, (((0,), (1,)), ((), ())), precision=HIGHEST, preferred_element_type=f32
    )
    values[...] = sample_weight_ref[...] * (cleaned_ref[...] - fitted)
    totals[...] = jnp.zeros_like(totals)
    accumulate(values, coarse_ref, fine_ref, totals, 0, GROUPS)
    for kind, source_ref in enumerate((totals, weight_totals_ref)):
        for column in range(2):
            halves[...] = source_ref[:, column * LANES : (column + 1) * LANES]
            for half in range(2):
                out_ref[half * 2 + column, kind * HIT : (kind + 1) * HIT, :] = halves[pl.ds(half, HIT, stride=2), :]


def route_kernel(first_ref, second_ref, third_ref, fourth_ref, slot_ref, out_ref):
    total = first_ref[...] + second_ref[...] + third_ref[...] + fourth_ref[...]
    row = lax.broadcasted_iota(jnp.int32, (SPANS * CHUNK, 2 * HIT), 0)
    selector = jnp.where(row == slot_ref[...], 1.0, 0.0).astype(bf16)
    out_ref[...] = exact_left_dot(selector, total)


def merge_kernel(received_ref, tile_ref, rhs_ref, weight_ref):
    rows = SPANS * CHUNK
    wanted = lax.broadcasted_iota(jnp.int32, (16, rows), 0)
    column = lax.broadcasted_iota(jnp.int32, (16, rows), 1)
    chosen = (tile_ref[...] == wanted % 8) & ((column % CHUNK) // 2 == wanted // 8)
    selector = jnp.where(chosen, 1.0, 0.0).astype(bf16)
    merged = exact_left_dot(selector, received_ref[...])
    rhs_ref[...] = merged[0:8, :]
    weight_ref[...] = merged[8:16, :]


def shape(*dims, dtype=f32):
    return jax.ShapeDtypeStruct(dims, dtype)


def exchange(values, axes, *dims):
    return lax.all_to_all(values.reshape(dims), axes, split_axis=0, concat_axis=0, tiled=True)


def body(timestream, templates, bias_group, det_weight, cut_start, cut_len, pointing, hit_tiles):
    span = ("depth", "plane")
    own = lax.axis_index(span)
    outgoing = call(pack_kernel, shape(SPANS * SENT, LANES), "pack", [VMEM, VMEM], vmem=60)(timestream, templates)
    received = exchange(outgoing, span, SPANS, 1, SENT * LANES).reshape(SPANS * SENT, LANES)

    groups = bias_group.reshape(DEPTH, PLANE, DEV_DETS).transpose(2, 1, 0).reshape(WAFER_DETS)
    coarse, fine, sample_weight = call(
        prepare_kernel,
        (shape(SPAN_LEN, WAFER_DETS), shape(GROUPS, WAFER_DETS, GROUP_TIMES), shape(SPAN_LEN, WAFER_DETS)),
        "prepare", [SMEM, VMEM] + [ANY] * 4,
        [
            pltpu.VMEM((WAFER_DETS,), f32), pltpu.VMEM((WAFER_DETS,), jnp.int32), pltpu.VMEM((WAFER_DETS,), jnp.int32),
            pltpu.SemaphoreType.DMA((3,)),
        ],
    )(own.reshape(1), pointing, det_weight, cut_start, cut_len, outgoing)
    weight_totals = call(weight_first_kernel, shape(LANES, 2 * LANES), "weight_first", [VMEM] * 3, vmem=24)(
        sample_weight, coarse, fine
    )
    order = jnp.arange(HIT, dtype=jnp.int32)
    own_owner = lax.dynamic_index_in_dim(hit_tiles, own, 0, keepdims=False) // TILE_OWN
    earlier = (own_owner[None, :] == own_owner[:, None]) & (order[None, :] < order[:, None])
    base = own_owner * CHUNK + jnp.sum(earlier.astype(jnp.int32), axis=1)
    slot = jnp.concatenate([base, base + 2])[None, :]
    mine = hit_tiles // TILE_OWN == own
    position = jnp.broadcast_to(order[None, :], (SPANS, HIT))
    first = jnp.min(jnp.where(mine, position, HIT), axis=1, keepdims=True)
    last = jnp.max(jnp.where(mine, position, -1), axis=1, keepdims=True)
    within = hit_tiles % TILE_OWN + 1
    first_tile = jnp.sum(jnp.where(position == first, within, 0), axis=1) - 1
    last_tile = jnp.sum(jnp.where(position == last, within, 0), axis=1) - 1
    slot_tile = jnp.stack([first_tile, last_tile, first_tile, last_tile], axis=1).reshape(1, SPANS * CHUNK)

    partial = call(project_kernel, shape(SPANS * CHUNK, LANES), "project", [VMEM] * 3 + [ANY])(
        received, groups[None, :], templates, weight_totals
    )
    reduced = exchange(partial, "plane", PLANE, DEPTH * CHUNK, LANES).reshape(SPANS * CHUNK, LANES)
    cleaned = call(clean_kernel, shape(SPAN_LEN, WAFER_DETS), "clean", [VMEM] * 3 + [ANY])(
        received, groups[:, None], bias_group[None, :], partial
    )
    reduced = call(plane_total_kernel, shape(SPANS * CHUNK, LANES), "plane_total", [VMEM, ANY])(reduced, cleaned)
    weight_totals = call(weight_rest_kernel, shape(LANES, 2 * LANES), "weight_rest", [VMEM] * 4 + [ANY], vmem=24)(
        sample_weight, coarse, fine, weight_totals, reduced
    )
    reduced = exchange(reduced, "depth", DEPTH, PLANE * CHUNK, LANES).reshape(SPANS * CHUNK, LANES)
    totals = call(depth_total_kernel, shape(SPANS * CHUNK, LANES), "depth_total", [VMEM, ANY])(reduced, weight_totals)
    gathered = exchange(totals, "plane", PLANE, DEPTH * CHUNK, LANES).reshape(SPANS * CHUNK, LANES)
    inverse = call(factor_kernel, shape(LANES, LANES), "factor", [VMEM])(reduced)
    coeffs, tiles = call(
        bin_kernel, (shape(SPANS * CHUNK, LANES), shape(WAFERS, 2 * HIT, LANES)), "bin", [VMEM] * 8,
        [
            pltpu.VMEM((SPAN_LEN, WAFER_DETS), f32), pltpu.VMEM((LANES, 2 * LANES), f32),
            pltpu.VMEM((LANES, LANES), f32),
        ],
        vmem=24,
    )(gathered, inverse, templates, cleaned, sample_weight, coarse, fine, weight_totals)
    own_wafer = lax.axis_index("wafer")
    tiles = [
        lax.ppermute(
            lax.dynamic_index_in_dim(tiles, (own_wafer + k) % WAFERS, 0, keepdims=False), "wafer",
            [(w, (w + k) % WAFERS) for w in range(WAFERS)],
        ) if k else lax.dynamic_index_in_dim(tiles, own_wafer, 0, keepdims=False)
        for k in range(WAFERS)
    ]
    routed = call(route_kernel, shape(SPANS * CHUNK, LANES), "route", [VMEM] * 5)(*tiles, slot)
    routed = exchange(routed, span, SPANS, CHUNK, LANES).reshape(SPANS * CHUNK, LANES)
    own_place = lax.axis_index("plane") * DEPTH + lax.axis_index("depth")
    own_coeffs = lax.dynamic_slice_in_dim(coeffs, own_place * CHUNK, 3)
    fit_coeffs = jnp.concatenate([own_coeffs[:, :NT], own_coeffs[:, NT:]], axis=0)
    rhs_map, weight_map = call(merge_kernel, (shape(8, LANES), shape(8, LANES)), "merge", [VMEM, VMEM])(
        routed, slot_tile
    )
    return (fit_coeffs, rhs_map, weight_map)


def solution(mesh):
    mesh = jax.sharding.Mesh(mesh.devices.reshape(WAFERS, DEPTH, PLANE), ("wafer", "depth", "plane"))
    span = ("depth", "plane")
    in_specs = (
        P(("wafer", *span), None),
        P(None, span),
        P("wafer"),
        P("wafer"),
        P("wafer"),
        P("wafer"),
        P("wafer", span),
        P(),
    )
    out_specs = (P(("wafer", *span), None), P(span, "wafer"), P(span, "wafer"))
    return jax.shard_map(body, mesh=mesh, in_specs=in_specs, out_specs=out_specs, check_vma=False)
```

```python
import jax
import jax.numpy as jnp
from jax import lax
from jax.experimental import pallas as pl
from jax.experimental.pallas import tpu as pltpu
from jax.sharding import PartitionSpec as P

NGROUP = 12
TILE = 512
TILE_OWN = 8
SPANS = 64
WAFERS = 4
PLANE = 8
CORES = 2
ROWS = PLANE // CORES
DEPTH = SPANS // PLANE
DEV_DETS = 6
SENT = 2 * DEV_DETS + 1
WAFER_DETS = SPANS * DEV_DETS
SPAN_LEN = 256
NT = 64
HIT = 64
LANES = 128
CHUNK = 4
GROUPS = 4
FIRST_GROUPS = 3
GROUP_TIMES = SPAN_LEN // GROUPS

f32 = jnp.float32
bf16 = jnp.bfloat16
HIGHEST = lax.Precision.HIGHEST
VMEM = pl.BlockSpec(memory_space=pltpu.VMEM)
SMEM = pl.BlockSpec(memory_space=pltpu.SMEM)
ANY = pl.BlockSpec(memory_space=pl.ANY)


def call(kernel, out_shape, name, in_specs, scratch_shapes=(), vmem=16):
    return pl.pallas_call(
        kernel,
        out_shape=out_shape,
        in_specs=in_specs,
        out_specs=jax.tree.map(lambda unused: VMEM, out_shape),
        scratch_shapes=scratch_shapes,
        name=name,
        compiler_params=pltpu.CompilerParams(vmem_limit_bytes=vmem << 20),
        cost_estimate=pl.CostEstimate(flops=1 << 30, bytes_accessed=1 << 20, transcendentals=0),
    )


def split3(value):
    high = value.astype(bf16)
    rest = value - high.astype(f32)
    middle = rest.astype(bf16)
    low = (rest - middle.astype(f32)).astype(bf16)
    return high, middle, low


def exact_left_dot(left, right):
    return sum(jnp.dot(left, piece, preferred_element_type=f32) for piece in split3(right))


def pack_kernel(stream_ref, templates_ref, out_ref):
    templates = templates_ref[...]
    gram = lax.dot_general(
        templates, jnp.concatenate([templates, jnp.zeros_like(templates)], axis=0), (((1,), (1,)), ((), ())),
        precision=HIGHEST, preferred_element_type=f32,
    )
    for s in range(SPANS):
        for half in range(2):
            first = s * SPAN_LEN + half * LANES
            out_ref[pl.ds(s * SENT + half, DEV_DETS, stride=2), :] = stream_ref[:, first : first + LANES]
    out_ref[pl.ds(2 * DEV_DETS, SPANS, stride=SENT), :] = gram


def received_rows(received_ref):
    def rows(i, half):
        return jnp.concatenate(
            [received_ref[pl.ds(p * SENT + 2 * i + half, DEPTH, stride=PLANE * SENT), :] for p in range(PLANE)], axis=0
        )

    return jnp.concatenate(
        [jnp.concatenate([rows(i, 0), rows(i, 1)], axis=1) for i in range(DEV_DETS)], axis=0
    )


def lines(group_row):
    line = lax.broadcasted_iota(jnp.int32, (16, WAFER_DETS), 0)
    return jnp.where(line == group_row, 1.0, 0.0).astype(bf16)


def plane_total_kernel(received_ref, after_ref, out_ref):
    rows = DEPTH * CHUNK
    total = received_ref[0:rows, :]
    for k in range(1, PLANE):
        total = total + received_ref[rows * k : rows * (k + 1), :]
    gram_rows = received_ref[pl.ds(3, PLANE, stride=rows), :]
    for k in range(DEPTH):
        out_ref[rows * k : rows * (k + 1), :] = total
        out_ref[pl.ds(rows * k + 3, PLANE, stride=CHUNK), :] = gram_rows


def depth_total_kernel(received_ref, after_ref, out_ref):
    rows = DEPTH * CHUNK
    total = received_ref[0:rows, :]
    for k in range(1, DEPTH):
        total = total + received_ref[rows * k : rows * (k + 1), :]
    out_ref[...] = total


def factor_kernel(received_ref, templates_ref, out_ref, solved_ref):
    gram = received_ref[pl.ds(3, SPANS, stride=CHUNK), :]
    lane = lax.broadcasted_iota(jnp.int32, (NT, LANES), 1)
    row = lax.broadcasted_iota(jnp.int32, (NT, LANES), 0)
    work = jnp.where(lane < NT, gram, jnp.where(lane - NT == row, 1.0, 0.0))
    blocks = [work[8 * b : 8 * b + 8, :] for b in range(NT // 8)]
    sublane = lax.broadcasted_iota(jnp.int32, (8, LANES), 0)

    def lane_spread(block, k):
        return jnp.broadcast_to(block[:, k : k + 1], (8, LANES))

    for b in range(NT // 8):
        first = 8 * b
        rows = [jnp.broadcast_to(blocks[b][i : i + 1, :], (8, LANES)) for i in range(8)]
        corner = {(i, j): lane_spread(rows[i], first + j) for i in range(8) for j in range(i, 8)}
        columns = [[lane_spread(block, first + j) for block in blocks[b:]] for j in range(8)]
        for i in range(8):
            inverse = 1.0 / corner[i, i]
            ratios = [column * inverse for column in columns[i]]
            ratios[0] = jnp.where(sublane > i, ratios[0], 0.0)
            blocks[b:] = [block - ratio * rows[i] for block, ratio in zip(blocks[b:], ratios)]
            for j in range(i + 1, 8):
                shift = corner[i, j] * inverse
                rows[j] = rows[j] - shift * rows[i]
                columns[j] = [later - earlier * shift for later, earlier in zip(columns[j], columns[i])]
                for k in range(j, 8):
                    corner[j, k] = corner[j, k] - shift * corner[i, k]
    work = jnp.concatenate(blocks, axis=0)
    pivots = jnp.sum(jnp.where(lane == row, work, 0.0), axis=1, keepdims=True)
    inverse = work * lax.rsqrt(pivots)
    swapped = pltpu.roll(inverse, NT, 1)
    out_ref[...] = jnp.where(lane < NT, swapped, 0.0)
    solved_ref[...] = jnp.dot(
        swapped[:, :NT], templates_ref[...], precision=HIGHEST, preferred_element_type=f32
    )


def prepare_kernel(
    own_ref, pointing_ref, weight_hbm, start_hbm, length_hbm, after_ref, coarse_ref, fine_ref, sample_weight_ref,
    weight_ref, start_ref, length_ref, semaphores
):
    copies = [
        pltpu.make_async_copy(source, target, semaphores.at[k])
        for k, (source, target) in enumerate(
            ((weight_hbm, weight_ref), (start_hbm, start_ref), (length_hbm, length_ref))
        )
    ]
    for copy in copies:
        copy.start()
    pointing = pointing_ref[...]
    coarse_ref[...] = (pointing >> 8).astype(f32).T
    fine = (pointing & 255).astype(f32)
    for g in range(GROUPS):
        fine_ref[g] = fine[:, g * GROUP_TIMES : (g + 1) * GROUP_TIMES]
    time = lax.broadcasted_iota(jnp.int32, (SPAN_LEN, WAFER_DETS), 0) + own_ref[0] * SPAN_LEN
    for copy in copies:
        copy.wait()
    start = start_ref[...].reshape(1, WAFER_DETS)
    stop = start + length_ref[...].reshape(1, WAFER_DETS)
    inside = (time >= start) & (time < stop)
    weight = jnp.broadcast_to(weight_ref[...].reshape(1, WAFER_DETS), (SPAN_LEN, WAFER_DETS))
    sample_weight_ref[...] = jnp.where(inside, 0.0, weight).astype(bf16).astype(f32)


def project_kernel(received_ref, group_ref, templates_ref, after_ref, out_ref):
    templates = templates_ref[...]
    raw = lax.dot_general(
        received_rows(received_ref), jnp.concatenate([templates, templates], axis=0), (((1,), (1,)), ((), ())),
        precision=HIGHEST, preferred_element_type=f32,
    )
    onehot = lines(group_ref[...])
    means = exact_left_dot(onehot, raw) * (NGROUP / WAFER_DETS)
    mixed = raw - sum(
        lax.dot_general(onehot, piece, (((0,), (0,)), ((), ())), preferred_element_type=f32) for piece in split3(means)
    )
    first_half = lax.broadcasted_iota(jnp.int32, (SPANS, LANES), 1) < NT
    for r in range(3):
        out_ref[pl.ds(r, SPANS, stride=CHUNK), :] = jnp.where(
            first_half, mixed[r * SPANS : (r + 1) * SPANS], mixed[(r + 3) * SPANS : (r + 4) * SPANS]
        )
    gram_row = jnp.sum(received_ref[pl.ds(2 * DEV_DETS, SPANS, stride=SENT), :], axis=0, keepdims=True)
    out_ref[pl.ds(3, SPANS, stride=CHUNK), :] = jnp.broadcast_to(gram_row, (SPANS, LANES))


def clean_kernel(received_ref, column_ref, row_ref, after_ref, out_ref):
    row = lax.broadcasted_iota(jnp.int32, (WAFER_DETS, WAFER_DETS), 0)
    column = lax.broadcasted_iota(jnp.int32, (WAFER_DETS, WAFER_DETS), 1)
    det = ((row % DEPTH) * PLANE + (row % SPANS) // DEPTH) * DEV_DETS + row // SPANS
    keep = jnp.where(det == column, 1.0, 0.0)
    mixer = (keep - jnp.where(column_ref[...] == row_ref[...], NGROUP / WAFER_DETS, 0.0)).astype(bf16)
    out_ref[...] = sum(
        lax.dot_general(piece, mixer, (((0,), (0,)), ((), ())), preferred_element_type=f32)
        for piece in split3(received_rows(received_ref))
    )


def accumulate(values_ref, coarse_ref, fine_ref, totals_ref, first, last):
    labels = lax.broadcasted_iota(jnp.int32, (LANES, WAFER_DETS), 0).astype(f32).astype(bf16)
    lane = lax.broadcasted_iota(jnp.int32, (WAFER_DETS, LANES), 1)
    low_lane, high_lane = lane.astype(f32).astype(bf16), (lane + LANES).astype(f32).astype(bf16)
    one, zero = jnp.ones((WAFER_DETS, LANES), bf16), jnp.zeros((WAFER_DETS, LANES), bf16)
    blank = jnp.zeros((16, WAFER_DETS), bf16)

    def spread(rows, i):
        return jnp.broadcast_to(rows[i : i + 1], (16, WAFER_DETS)).astype(bf16)

    def step(g, carry):
        fine = fine_ref[g]
        left, right = [], []
        for block in range(GROUP_TIMES // 8):
            times = pl.ds(pl.multiple_of(g * GROUP_TIMES + 8 * block, 8), 8)
            coarse_rows, value_rows = coarse_ref[times, :], values_ref[times, :]
            for i in range(8):
                coarse, value = spread(coarse_rows, i), spread(value_rows, i)
                left.append(
                    jnp.concatenate(
                        [jnp.where(labels[16 * m : 16 * m + 16] == coarse, value, blank) for m in range(8)], axis=0
                    )
                )
                t = 8 * block + i
                point = jnp.broadcast_to(fine[:, t : t + 1], (WAFER_DETS, LANES)).astype(bf16)
                right.append(
                    jnp.concatenate(
                        [jnp.where(low_lane == point, one, zero), jnp.where(high_lane == point, one, zero)], axis=1
                    )
                )
        totals_ref[...] += jnp.dot(
            jnp.concatenate(left, axis=1), jnp.concatenate(right, axis=0), preferred_element_type=f32
        )
        return carry

    lax.fori_loop(first, last, step, 0)


def weight_first_kernel(sample_weight_ref, coarse_ref, fine_ref, out_ref):
    out_ref[...] = jnp.zeros_like(out_ref)
    accumulate(sample_weight_ref, coarse_ref, fine_ref, out_ref, 0, FIRST_GROUPS)


def weight_rest_kernel(sample_weight_ref, coarse_ref, fine_ref, totals_ref, after_ref, out_ref):
    out_ref[...] = totals_ref[...]
    accumulate(sample_weight_ref, coarse_ref, fine_ref, out_ref, FIRST_GROUPS, GROUPS)


def bin_kernel(
    place_ref, first_ref, second_ref, third_ref, fourth_ref, inverse_ref, solved_ref, cleaned_ref, sample_weight_ref,
    coarse_ref, fine_ref, weight_totals_ref, out_ref, values, totals, halves, ordered
):
    for k, pair_ref in enumerate((first_ref, second_ref, third_ref, fourth_ref)):
        for j in range(CORES):
            start = place_ref[k * CORES + j] * DEV_DETS
            for r in range(3):
                rows = pair_ref[pl.ds(j * DEPTH * CHUNK + r, DEPTH, stride=CHUNK), :]
                for half in range(2):
                    target = pl.ds(start + (half * 3 + r), DEPTH, stride=PLANE * DEV_DETS)
                    ordered[target, :] = pltpu.roll(rows, NT, 1) if half else rows
    middle = lax.dot_general(
        ordered[...], inverse_ref[...], (((1,), (1,)), ((), ())), precision=HIGHEST, preferred_element_type=f32
    )
    fitted = lax.dot_general(
        solved_ref[...], middle, (((0,), (1,)), ((), ())), precision=HIGHEST, preferred_element_type=f32
    )
    values[...] = sample_weight_ref[...] * (cleaned_ref[...] - fitted)
    totals[...] = jnp.zeros_like(totals)
    accumulate(values, coarse_ref, fine_ref, totals, 0, GROUPS)
    for kind, source_ref in enumerate((totals, weight_totals_ref)):
        for column in range(2):
            halves[...] = source_ref[:, column * LANES : (column + 1) * LANES]
            for half in range(2):
                out_ref[half * 2 + column, kind * HIT : (kind + 1) * HIT, :] = halves[pl.ds(half, HIT, stride=2), :]


def coeffs_kernel(gathered_ref, inverse_ref, after_ref, out_ref):
    inverse = inverse_ref[:, :NT]
    gathered = gathered_ref[...]
    for half in range(2):
        middle = lax.dot_general(
            gathered[:, half * NT : half * NT + NT], inverse, (((1,), (1,)), ((), ())),
            precision=HIGHEST, preferred_element_type=f32,
        )
        coeffs = jnp.dot(middle, inverse, precision=HIGHEST, preferred_element_type=f32)
        out_ref[half * 3 : half * 3 + 3, :] = coeffs[0:3, :]


def route_kernel(first_ref, second_ref, third_ref, fourth_ref, slot_ref, out_ref):
    total = first_ref[...] + second_ref[...] + third_ref[...] + fourth_ref[...]
    row = lax.broadcasted_iota(jnp.int32, (SPANS * CHUNK, 2 * HIT), 0)
    selector = jnp.where(row == slot_ref[...], 1.0, 0.0).astype(bf16)
    out_ref[...] = exact_left_dot(selector, total)


def merge_kernel(received_ref, tile_ref, rhs_ref, weight_ref):
    rows = SPANS * CHUNK
    wanted = lax.broadcasted_iota(jnp.int32, (16, rows), 0)
    column = lax.broadcasted_iota(jnp.int32, (16, rows), 1)
    chosen = (tile_ref[...] == wanted % 8) & ((column % CHUNK) // 2 == wanted // 8)
    selector = jnp.where(chosen, 1.0, 0.0).astype(bf16)
    merged = exact_left_dot(selector, received_ref[...])
    rhs_ref[...] = merged[0:8, :]
    weight_ref[...] = merged[8:16, :]


def shape(*dims, dtype=f32):
    return jax.ShapeDtypeStruct(dims, dtype)


def exchange(values, axes, *dims):
    return lax.all_to_all(values.reshape(dims), axes, split_axis=0, concat_axis=0, tiled=True)


def body(timestream, templates, bias_group, det_weight, cut_start, cut_len, pointing, hit_tiles):
    plane = ("row", "core")
    span = ("depth", *plane)
    own = lax.axis_index(span)
    outgoing = call(pack_kernel, shape(SPANS * SENT, LANES), "pack", [VMEM, VMEM], vmem=60)(timestream, templates)
    received = exchange(outgoing, span, SPANS, 1, SENT * LANES).reshape(SPANS * SENT, LANES)

    groups = bias_group.reshape(DEPTH, PLANE, DEV_DETS).transpose(2, 1, 0).reshape(WAFER_DETS)
    coarse, fine, sample_weight = call(
        prepare_kernel,
        (shape(SPAN_LEN, WAFER_DETS), shape(GROUPS, WAFER_DETS, GROUP_TIMES), shape(SPAN_LEN, WAFER_DETS)),
        "prepare", [SMEM, VMEM] + [ANY] * 4,
        [
            pltpu.VMEM((WAFER_DETS,), f32), pltpu.VMEM((WAFER_DETS,), jnp.int32), pltpu.VMEM((WAFER_DETS,), jnp.int32),
            pltpu.SemaphoreType.DMA((3,)),
        ],
    )(own.reshape(1), pointing, det_weight, cut_start, cut_len, outgoing)
    weight_totals = call(weight_first_kernel, shape(LANES, 2 * LANES), "weight_first", [VMEM] * 3, vmem=24)(
        sample_weight, coarse, fine
    )
    order = jnp.arange(HIT, dtype=jnp.int32)
    own_owner = lax.dynamic_index_in_dim(hit_tiles, own, 0, keepdims=False) // TILE_OWN
    earlier = (own_owner[None, :] == own_owner[:, None]) & (order[None, :] < order[:, None])
    base = own_owner * CHUNK + jnp.sum(earlier.astype(jnp.int32), axis=1)
    slot = jnp.concatenate([base, base + 2])[None, :]
    mine = hit_tiles // TILE_OWN == own
    position = jnp.broadcast_to(order[None, :], (SPANS, HIT))
    first = jnp.min(jnp.where(mine, position, HIT), axis=1, keepdims=True)
    last = jnp.max(jnp.where(mine, position, -1), axis=1, keepdims=True)
    within = hit_tiles % TILE_OWN + 1
    first_tile = jnp.sum(jnp.where(position == first, within, 0), axis=1) - 1
    last_tile = jnp.sum(jnp.where(position == last, within, 0), axis=1) - 1
    slot_tile = jnp.stack([first_tile, last_tile, first_tile, last_tile], axis=1).reshape(1, SPANS * CHUNK)

    partial = call(project_kernel, shape(SPANS * CHUNK, LANES), "project", [VMEM] * 3 + [ANY])(
        received, groups[None, :], templates, weight_totals
    )
    reduced = exchange(partial, plane, PLANE, DEPTH * CHUNK, LANES).reshape(SPANS * CHUNK, LANES)
    cleaned = call(clean_kernel, shape(SPAN_LEN, WAFER_DETS), "clean", [VMEM] * 3 + [ANY])(
        received, groups[:, None], bias_group[None, :], partial
    )
    reduced = call(plane_total_kernel, shape(SPANS * CHUNK, LANES), "plane_total", [VMEM, ANY])(reduced, cleaned)
    weight_totals = call(weight_rest_kernel, shape(LANES, 2 * LANES), "weight_rest", [VMEM] * 4 + [ANY], vmem=24)(
        sample_weight, coarse, fine, weight_totals, reduced
    )
    reduced = exchange(reduced, "depth", DEPTH, PLANE * CHUNK, LANES).reshape(SPANS * CHUNK, LANES)
    totals = call(depth_total_kernel, shape(DEPTH * CHUNK, LANES), "depth_total", [VMEM, ANY])(reduced, weight_totals)
    partner = lax.ppermute(totals, "core", [(0, 1), (1, 0)])
    pair = jnp.concatenate([totals, partner], axis=0)
    pairs = [pair] + [
        lax.ppermute(pair, "row", [(x, (x + k) % ROWS) for x in range(ROWS)]) for k in (2, 1, 3)
    ]
    own_row, own_core = lax.axis_index("row"), lax.axis_index("core")
    places = jnp.stack(
        [(own_row + ROWS - k) % ROWS * CORES + (own_core + j) % CORES for k in (0, 2, 1, 3) for j in range(CORES)]
    )
    inverse, solved = call(factor_kernel, (shape(NT, LANES), shape(NT, SPAN_LEN)), "factor", [VMEM] * 2)(
        reduced, templates
    )
    tiles = call(
        bin_kernel, shape(WAFERS, 2 * HIT, LANES), "bin", [SMEM] + [VMEM] * 11,
        [
            pltpu.VMEM((SPAN_LEN, WAFER_DETS), f32), pltpu.VMEM((LANES, 2 * LANES), f32),
            pltpu.VMEM((LANES, LANES), f32), pltpu.VMEM((WAFER_DETS, LANES), f32),
        ],
        vmem=24,
    )(places, *pairs, inverse, solved, cleaned, sample_weight, coarse, fine, weight_totals)
    own_wafer = lax.axis_index("wafer")
    tiles = [
        lax.ppermute(
            lax.dynamic_index_in_dim(tiles, (own_wafer + k) % WAFERS, 0, keepdims=False), "wafer",
            [(w, (w + k) % WAFERS) for w in range(WAFERS)],
        ) if k else lax.dynamic_index_in_dim(tiles, own_wafer, 0, keepdims=False)
        for k in (0, 2, 1, 3)
    ]
    routed = call(route_kernel, shape(SPANS * CHUNK, LANES), "route", [VMEM] * 5)(*tiles, slot)
    sent = routed
    routed = exchange(routed, span, SPANS, CHUNK, LANES).reshape(SPANS * CHUNK, LANES)
    own_rows = lax.dynamic_slice_in_dim(totals, lax.axis_index("depth") * CHUNK, CHUNK)
    own_rows = jnp.concatenate([own_rows, own_rows], axis=0)
    fit_coeffs = call(coeffs_kernel, shape(DEV_DETS, NT), "coeffs", [VMEM] * 2 + [ANY])(own_rows, inverse, sent)
    rhs_map, weight_map = call(merge_kernel, (shape(8, LANES), shape(8, LANES)), "merge", [VMEM, VMEM])(
        routed, slot_tile
    )
    return (fit_coeffs, rhs_map, weight_map)


def solution(mesh):
    mesh = jax.sharding.Mesh(mesh.devices.reshape(WAFERS, DEPTH, ROWS, CORES), ("wafer", "depth", "row", "core"))
    span = ("depth", "row", "core")
    in_specs = (
        P(("wafer", *span), None),
        P(None, span),
        P("wafer"),
        P("wafer"),
        P("wafer"),
        P("wafer"),
        P("wafer", span),
        P(),
    )
    out_specs = (P(("wafer", *span), None), P(span, "wafer"), P(span, "wafer"))
    return jax.shard_map(body, mesh=mesh, in_specs=in_specs, out_specs=out_specs, check_vma=False)
```

```python
import jax
import jax.numpy as jnp
from jax import lax
from jax.experimental import pallas as pl
from jax.experimental.pallas import tpu as pltpu
from jax.sharding import PartitionSpec as P

NGROUP = 12
TILE = 512
TILE_OWN = 8
SPANS = 64
WAFERS = 4
PLANE = 8
CORES = 2
ROWS = PLANE // CORES
DEPTH = SPANS // PLANE
DEV_DETS = 6
SENT = 2 * DEV_DETS + 1
WAFER_DETS = SPANS * DEV_DETS
SPAN_LEN = 256
NT = 64
HIT = 64
LANES = 128
CHUNK = 4
GROUPS = 4
FIRST_GROUPS = 3
GROUP_TIMES = SPAN_LEN // GROUPS

f32 = jnp.float32
bf16 = jnp.bfloat16
HIGHEST = lax.Precision.HIGHEST
VMEM = pl.BlockSpec(memory_space=pltpu.VMEM)
SMEM = pl.BlockSpec(memory_space=pltpu.SMEM)
ANY = pl.BlockSpec(memory_space=pl.ANY)


def call(kernel, out_shape, name, in_specs, scratch_shapes=(), vmem=16):
    return pl.pallas_call(
        kernel,
        out_shape=out_shape,
        in_specs=in_specs,
        out_specs=jax.tree.map(lambda unused: VMEM, out_shape),
        scratch_shapes=scratch_shapes,
        name=name,
        compiler_params=pltpu.CompilerParams(vmem_limit_bytes=vmem << 20),
        cost_estimate=pl.CostEstimate(flops=1 << 30, bytes_accessed=1 << 20, transcendentals=0),
    )


def split3(value):
    high = value.astype(bf16)
    rest = value - high.astype(f32)
    middle = rest.astype(bf16)
    low = (rest - middle.astype(f32)).astype(bf16)
    return high, middle, low


def exact_left_dot(left, right):
    return sum(jnp.dot(left, piece, preferred_element_type=f32) for piece in split3(right))


def pack_kernel(stream_ref, templates_ref, out_ref):
    templates = templates_ref[...]
    gram = lax.dot_general(
        templates, jnp.concatenate([templates, jnp.zeros_like(templates)], axis=0), (((1,), (1,)), ((), ())),
        precision=HIGHEST, preferred_element_type=f32,
    )
    for s in range(SPANS):
        for half in range(2):
            first = s * SPAN_LEN + half * LANES
            out_ref[pl.ds(s * SENT + half, DEV_DETS, stride=2), :] = stream_ref[:, first : first + LANES]
    out_ref[pl.ds(2 * DEV_DETS, SPANS, stride=SENT), :] = gram


def received_rows(received_ref):
    def rows(i, half):
        return jnp.concatenate(
            [received_ref[pl.ds(p * SENT + 2 * i + half, DEPTH, stride=PLANE * SENT), :] for p in range(PLANE)], axis=0
        )

    return jnp.concatenate(
        [jnp.concatenate([rows(i, 0), rows(i, 1)], axis=1) for i in range(DEV_DETS)], axis=0
    )


def lines(group_row):
    line = lax.broadcasted_iota(jnp.int32, (16, WAFER_DETS), 0)
    return jnp.where(line == group_row, 1.0, 0.0).astype(bf16)


def plane_total_kernel(received_ref, after_ref, out_ref):
    rows = DEPTH * CHUNK
    total = received_ref[0:rows, :]
    for k in range(1, PLANE):
        total = total + received_ref[rows * k : rows * (k + 1), :]
    gram_rows = received_ref[pl.ds(3, PLANE, stride=rows), :]
    for k in range(DEPTH):
        out_ref[rows * k : rows * (k + 1), :] = total
        out_ref[pl.ds(rows * k + 3, PLANE, stride=CHUNK), :] = gram_rows


def depth_total_kernel(received_ref, after_ref, out_ref):
    rows = DEPTH * CHUNK
    total = received_ref[0:rows, :]
    for k in range(1, DEPTH):
        total = total + received_ref[rows * k : rows * (k + 1), :]
    out_ref[...] = total


def factor_kernel(received_ref, templates_ref, after_ref, out_ref, solved_ref):
    gram = received_ref[pl.ds(3, SPANS, stride=CHUNK), :]
    lane = lax.broadcasted_iota(jnp.int32, (NT, LANES), 1)
    row = lax.broadcasted_iota(jnp.int32, (NT, LANES), 0)
    work = jnp.where(lane < NT, gram, jnp.where(lane - NT == row, 1.0, 0.0))
    blocks = [work[8 * b : 8 * b + 8, :] for b in range(NT // 8)]
    sublane = lax.broadcasted_iota(jnp.int32, (8, LANES), 0)

    def lane_spread(block, k):
        return jnp.broadcast_to(block[:, k : k + 1], (8, LANES))

    for b in range(NT // 8):
        first = 8 * b
        rows = [jnp.broadcast_to(blocks[b][i : i + 1, :], (8, LANES)) for i in range(8)]
        corner = {(i, j): lane_spread(rows[i], first + j) for i in range(8) for j in range(i, 8)}
        columns = [[lane_spread(block, first + j) for block in blocks[b:]] for j in range(8)]
        for i in range(8):
            inverse = 1.0 / corner[i, i]
            ratios = [column * inverse for column in columns[i]]
            ratios[0] = jnp.where(sublane > i, ratios[0], 0.0)
            blocks[b:] = [block - ratio * rows[i] for block, ratio in zip(blocks[b:], ratios)]
            for j in range(i + 1, 8):
                shift = corner[i, j] * inverse
                rows[j] = rows[j] - shift * rows[i]
                columns[j] = [later - earlier * shift for later, earlier in zip(columns[j], columns[i])]
                for k in range(j, 8):
                    corner[j, k] = corner[j, k] - shift * corner[i, k]
    work = jnp.concatenate(blocks, axis=0)
    pivots = jnp.sum(jnp.where(lane == row, work, 0.0), axis=1, keepdims=True)
    inverse = work * lax.rsqrt(pivots)
    swapped = pltpu.roll(inverse, NT, 1)
    out_ref[...] = jnp.where(lane < NT, swapped, 0.0)
    solved_ref[...] = jnp.dot(
        swapped[:, :NT], templates_ref[...], precision=HIGHEST, preferred_element_type=f32
    )


def prepare_kernel(
    own_ref, pointing_ref, weight_hbm, start_hbm, length_hbm, after_ref, coarse_ref, fine_ref, sample_weight_ref,
    weight_ref, start_ref, length_ref, semaphores
):
    copies = [
        pltpu.make_async_copy(source, target, semaphores.at[k])
        for k, (source, target) in enumerate(
            ((weight_hbm, weight_ref), (start_hbm, start_ref), (length_hbm, length_ref))
        )
    ]
    for copy in copies:
        copy.start()
    pointing = pointing_ref[...]
    coarse_ref[...] = (pointing >> 8).astype(f32).T
    fine = (pointing & 255).astype(f32)
    for g in range(GROUPS):
        fine_ref[g] = fine[:, g * GROUP_TIMES : (g + 1) * GROUP_TIMES]
    time = lax.broadcasted_iota(jnp.int32, (SPAN_LEN, WAFER_DETS), 0) + own_ref[0] * SPAN_LEN
    for copy in copies:
        copy.wait()
    start = start_ref[...].reshape(1, WAFER_DETS)
    stop = start + length_ref[...].reshape(1, WAFER_DETS)
    inside = (time >= start) & (time < stop)
    weight = jnp.broadcast_to(weight_ref[...].reshape(1, WAFER_DETS), (SPAN_LEN, WAFER_DETS))
    sample_weight_ref[...] = jnp.where(inside, 0.0, weight).astype(bf16).astype(f32)


def project_kernel(received_ref, group_ref, templates_ref, after_ref, out_ref):
    templates = templates_ref[...]
    twice = jnp.concatenate([templates, templates], axis=0)
    received = received_rows(received_ref)

    def project(rows):
        return lax.dot_general(
            rows, twice, (((1,), (1,)), ((), ())), precision=HIGHEST, preferred_element_type=f32
        )

    raw = project(received)
    onehot = lines(group_ref[...])
    means = project(exact_left_dot(onehot, received) * (NGROUP / WAFER_DETS))
    mixed = raw - sum(
        lax.dot_general(onehot, piece, (((0,), (0,)), ((), ())), preferred_element_type=f32) for piece in split3(means)
    )
    first_half = lax.broadcasted_iota(jnp.int32, (SPANS, LANES), 1) < NT
    for r in range(3):
        out_ref[pl.ds(r, SPANS, stride=CHUNK), :] = jnp.where(
            first_half, mixed[r * SPANS : (r + 1) * SPANS], mixed[(r + 3) * SPANS : (r + 4) * SPANS]
        )
    gram_row = jnp.sum(received_ref[pl.ds(2 * DEV_DETS, SPANS, stride=SENT), :], axis=0, keepdims=True)
    out_ref[pl.ds(3, SPANS, stride=CHUNK), :] = jnp.broadcast_to(gram_row, (SPANS, LANES))


def clean_kernel(received_ref, column_ref, row_ref, after_ref, out_ref):
    row = lax.broadcasted_iota(jnp.int32, (WAFER_DETS, WAFER_DETS), 0)
    column = lax.broadcasted_iota(jnp.int32, (WAFER_DETS, WAFER_DETS), 1)
    det = ((row % DEPTH) * PLANE + (row % SPANS) // DEPTH) * DEV_DETS + row // SPANS
    keep = jnp.where(det == column, 1.0, 0.0)
    mixer = (keep - jnp.where(column_ref[...] == row_ref[...], NGROUP / WAFER_DETS, 0.0)).astype(bf16)
    out_ref[...] = sum(
        lax.dot_general(piece, mixer, (((0,), (0,)), ((), ())), preferred_element_type=f32)
        for piece in split3(received_rows(received_ref))
    )


def accumulate(values_ref, coarse_ref, fine_ref, totals_ref, first, last, unroll=1):
    labels = lax.broadcasted_iota(jnp.int32, (LANES, WAFER_DETS), 0).astype(f32).astype(bf16)
    lane = lax.broadcasted_iota(jnp.int32, (WAFER_DETS, LANES), 1)
    low_lane, high_lane = lane.astype(f32).astype(bf16), (lane + LANES).astype(f32).astype(bf16)
    one, zero = jnp.ones((WAFER_DETS, LANES), bf16), jnp.zeros((WAFER_DETS, LANES), bf16)
    blank = jnp.zeros((16, WAFER_DETS), bf16)

    def spread(rows, i):
        return jnp.broadcast_to(rows[i : i + 1], (16, WAFER_DETS)).astype(bf16)

    def step(g, carry):
        fine = fine_ref[g]
        left, right = [], []
        for block in range(GROUP_TIMES // 8):
            times = pl.ds(pl.multiple_of(g * GROUP_TIMES + 8 * block, 8), 8)
            coarse_rows, value_rows = coarse_ref[times, :], values_ref[times, :]
            for i in range(8):
                coarse, value = spread(coarse_rows, i), spread(value_rows, i)
                left.append(
                    jnp.concatenate(
                        [jnp.where(labels[16 * m : 16 * m + 16] == coarse, value, blank) for m in range(8)], axis=0
                    )
                )
                t = 8 * block + i
                point = jnp.broadcast_to(fine[:, t : t + 1], (WAFER_DETS, LANES)).astype(bf16)
                right.append(
                    jnp.concatenate(
                        [jnp.where(low_lane == point, one, zero), jnp.where(high_lane == point, one, zero)], axis=1
                    )
                )
        totals_ref[...] += jnp.dot(
            jnp.concatenate(left, axis=1), jnp.concatenate(right, axis=0), preferred_element_type=f32
        )
        return carry

    lax.fori_loop(first, last, step, 0, unroll=unroll)


def weight_first_kernel(sample_weight_ref, coarse_ref, fine_ref, out_ref):
    out_ref[...] = jnp.zeros_like(out_ref)
    accumulate(sample_weight_ref, coarse_ref, fine_ref, out_ref, 0, FIRST_GROUPS)


def weight_rest_kernel(sample_weight_ref, coarse_ref, fine_ref, totals_ref, after_ref, out_ref):
    out_ref[...] = totals_ref[...]
    accumulate(sample_weight_ref, coarse_ref, fine_ref, out_ref, FIRST_GROUPS, GROUPS)


def bin_kernel(
    place_ref, gathered_ref, inverse_ref, solved_ref, cleaned_ref, sample_weight_ref, coarse_ref, fine_ref,
    weight_totals_ref, out_ref, values, totals, halves, ordered
):
    for p in range(PLANE):
        block = place_ref[p]
        for r in range(3):
            rows = gathered_ref.at[block][pl.ds(r, DEPTH, stride=CHUNK), :]
            for half in range(2):
                target = pl.ds(p * DEV_DETS + half * 3 + r, DEPTH, stride=PLANE * DEV_DETS)
                ordered[target, :] = pltpu.roll(rows, NT, 1) if half else rows
    middle = lax.dot_general(
        ordered[...], inverse_ref[...], (((1,), (1,)), ((), ())), precision=HIGHEST, preferred_element_type=f32
    )
    fitted = lax.dot_general(
        solved_ref[...], middle, (((0,), (1,)), ((), ())), precision=HIGHEST, preferred_element_type=f32
    )
    values[...] = sample_weight_ref[...] * (cleaned_ref[...] - fitted)
    totals[...] = jnp.zeros_like(totals)
    accumulate(values, coarse_ref, fine_ref, totals, 0, GROUPS, unroll=2)
    for kind, source_ref in enumerate((totals, weight_totals_ref)):
        for column in range(2):
            halves[...] = source_ref[:, column * LANES : (column + 1) * LANES]
            for half in range(2):
                out_ref[half * 2 + column, kind * HIT : (kind + 1) * HIT, :] = halves[pl.ds(half, HIT, stride=2), :]


def coeffs_kernel(gathered_ref, inverse_ref, after_ref, out_ref):
    inverse = inverse_ref[:, :NT]
    gathered = gathered_ref[...]
    for half in range(2):
        middle = lax.dot_general(
            gathered[:, half * NT : half * NT + NT], inverse, (((1,), (1,)), ((), ())),
            precision=HIGHEST, preferred_element_type=f32,
        )
        coeffs = jnp.dot(middle, inverse, precision=HIGHEST, preferred_element_type=f32)
        out_ref[half * 3 : half * 3 + 3, :] = coeffs[0:3, :]


def route_kernel(first_ref, second_ref, third_ref, fourth_ref, slot_ref, out_ref):
    total = first_ref[...] + second_ref[...] + third_ref[...] + fourth_ref[...]
    row = lax.broadcasted_iota(jnp.int32, (SPANS * CHUNK, 2 * HIT), 0)
    selector = jnp.where(row == slot_ref[...], 1.0, 0.0).astype(bf16)
    out_ref[...] = exact_left_dot(selector, total)


def merge_kernel(received_ref, tile_ref, rhs_ref, weight_ref):
    rows = SPANS * CHUNK
    wanted = lax.broadcasted_iota(jnp.int32, (16, rows), 0)
    column = lax.broadcasted_iota(jnp.int32, (16, rows), 1)
    chosen = (tile_ref[...] == wanted % 8) & ((column % CHUNK) // 2 == wanted // 8)
    selector = jnp.where(chosen, 1.0, 0.0).astype(bf16)
    merged = exact_left_dot(selector, received_ref[...])
    rhs_ref[...] = merged[0:8, :]
    weight_ref[...] = merged[8:16, :]


def shape(*dims, dtype=f32):
    return jax.ShapeDtypeStruct(dims, dtype)


def exchange(values, axes, *dims):
    return lax.all_to_all(values.reshape(dims), axes, split_axis=0, concat_axis=0, tiled=True)


def body(timestream, templates, bias_group, det_weight, cut_start, cut_len, pointing, hit_tiles):
    plane = ("row", "core")
    span = ("depth", *plane)
    own = lax.axis_index(span)
    outgoing = call(pack_kernel, shape(SPANS * SENT, LANES), "pack", [VMEM, VMEM], vmem=60)(timestream, templates)
    received = exchange(outgoing, span, SPANS, 1, SENT * LANES).reshape(SPANS * SENT, LANES)

    groups = bias_group.reshape(DEPTH, PLANE, DEV_DETS).transpose(2, 1, 0).reshape(WAFER_DETS)
    coarse, fine, sample_weight = call(
        prepare_kernel,
        (shape(SPAN_LEN, WAFER_DETS), shape(GROUPS, WAFER_DETS, GROUP_TIMES), shape(SPAN_LEN, WAFER_DETS)),
        "prepare", [SMEM, VMEM] + [ANY] * 4,
        [
            pltpu.VMEM((WAFER_DETS,), f32), pltpu.VMEM((WAFER_DETS,), jnp.int32), pltpu.VMEM((WAFER_DETS,), jnp.int32),
            pltpu.SemaphoreType.DMA((3,)),
        ],
    )(own.reshape(1), pointing, det_weight, cut_start, cut_len, outgoing)
    weight_totals = call(weight_first_kernel, shape(LANES, 2 * LANES), "weight_first", [VMEM] * 3, vmem=24)(
        sample_weight, coarse, fine
    )
    order = jnp.arange(HIT, dtype=jnp.int32)
    own_owner = lax.dynamic_index_in_dim(hit_tiles, own, 0, keepdims=False) // TILE_OWN
    earlier = (own_owner[None, :] == own_owner[:, None]) & (order[None, :] < order[:, None])
    base = own_owner * CHUNK + jnp.sum(earlier.astype(jnp.int32), axis=1)
    slot = jnp.concatenate([base, base + 2])[None, :]
    mine = hit_tiles // TILE_OWN == own
    position = jnp.broadcast_to(order[None, :], (SPANS, HIT))
    first = jnp.min(jnp.where(mine, position, HIT), axis=1, keepdims=True)
    last = jnp.max(jnp.where(mine, position, -1), axis=1, keepdims=True)
    within = hit_tiles % TILE_OWN + 1
    first_tile = jnp.sum(jnp.where(position == first, within, 0), axis=1) - 1
    last_tile = jnp.sum(jnp.where(position == last, within, 0), axis=1) - 1
    slot_tile = jnp.stack([first_tile, last_tile, first_tile, last_tile], axis=1).reshape(1, SPANS * CHUNK)

    partial = call(project_kernel, shape(SPANS * CHUNK, LANES), "project", [VMEM] * 3 + [ANY])(
        received, groups[None, :], templates, weight_totals
    )
    reduced = exchange(partial, plane, PLANE, DEPTH * CHUNK, LANES).reshape(SPANS * CHUNK, LANES)
    cleaned = call(clean_kernel, shape(SPAN_LEN, WAFER_DETS), "clean", [VMEM] * 3 + [ANY])(
        received, groups[:, None], bias_group[None, :], partial
    )
    reduced = call(plane_total_kernel, shape(SPANS * CHUNK, LANES), "plane_total", [VMEM, ANY])(reduced, cleaned)
    weight_totals = call(weight_rest_kernel, shape(LANES, 2 * LANES), "weight_rest", [VMEM] * 4 + [ANY], vmem=24)(
        sample_weight, coarse, fine, weight_totals, reduced
    )
    reduced = exchange(reduced, "depth", DEPTH, PLANE * CHUNK, LANES).reshape(SPANS * CHUNK, LANES)
    totals = call(depth_total_kernel, shape(DEPTH * CHUNK, LANES), "depth_total", [VMEM, ANY])(reduced, weight_totals)
    partner = lax.ppermute(totals, "core", [(0, 1), (1, 0)])
    pair = jnp.concatenate([totals, partner], axis=0)
    pairs = [pair] + [
        lax.ppermute(pair, "row", [(x, (x + k) % ROWS) for x in range(ROWS)]) for k in (1, 2, 3)
    ]
    own_row, own_core = lax.axis_index("row"), lax.axis_index("core")
    gathered = jnp.concatenate(pairs, axis=0).reshape(PLANE, DEPTH * CHUNK, LANES)
    block = jnp.arange(PLANE, dtype=jnp.int32)
    places = (own_row + ROWS - block // CORES) % ROWS * CORES + (own_core + block) % CORES
    inverse, solved = call(factor_kernel, (shape(NT, LANES), shape(NT, SPAN_LEN)), "factor", [VMEM] * 2 + [ANY])(
        reduced, templates, pair
    )
    tiles = call(
        bin_kernel, shape(WAFERS, 2 * HIT, LANES), "bin", [SMEM] + [VMEM] * 8,
        [
            pltpu.VMEM((SPAN_LEN, WAFER_DETS), f32), pltpu.VMEM((LANES, 2 * LANES), f32),
            pltpu.VMEM((LANES, LANES), f32), pltpu.VMEM((WAFER_DETS, LANES), f32),
        ],
        vmem=24,
    )(places, gathered, inverse, solved, cleaned, sample_weight, coarse, fine, weight_totals)
    own_wafer = lax.axis_index("wafer")
    tiles = [
        lax.ppermute(
            lax.dynamic_index_in_dim(tiles, (own_wafer + k) % WAFERS, 0, keepdims=False), "wafer",
            [(w, (w + k) % WAFERS) for w in range(WAFERS)],
        ) if k else lax.dynamic_index_in_dim(tiles, own_wafer, 0, keepdims=False)
        for k in range(WAFERS)
    ]
    routed = call(route_kernel, shape(SPANS * CHUNK, LANES), "route", [VMEM] * 5)(*tiles, slot)
    sent = routed
    routed = exchange(routed, span, SPANS, CHUNK, LANES).reshape(SPANS * CHUNK, LANES)
    own_rows = lax.dynamic_slice_in_dim(totals, lax.axis_index("depth") * CHUNK, CHUNK)
    own_rows = jnp.concatenate([own_rows, own_rows], axis=0)
    fit_coeffs = call(coeffs_kernel, shape(DEV_DETS, NT), "coeffs", [VMEM] * 2 + [ANY])(own_rows, inverse, sent)
    rhs_map, weight_map = call(merge_kernel, (shape(8, LANES), shape(8, LANES)), "merge", [VMEM, VMEM])(
        routed, slot_tile
    )
    return (fit_coeffs, rhs_map, weight_map)


def solution(mesh):
    mesh = jax.sharding.Mesh(mesh.devices.reshape(WAFERS, DEPTH, ROWS, CORES), ("wafer", "depth", "row", "core"))
    span = ("depth", "row", "core")
    in_specs = (
        P(("wafer", *span), None),
        P(None, span),
        P("wafer"),
        P("wafer"),
        P("wafer"),
        P("wafer"),
        P("wafer", span),
        P(),
    )
    out_specs = (P(("wafer", *span), None), P(span, "wafer"), P(span, "wafer"))
    return jax.shard_map(body, mesh=mesh, in_specs=in_specs, out_specs=out_specs, check_vma=False)
```

```python
import jax
import jax.numpy as jnp
from jax import lax
from jax.experimental import pallas as pl
from jax.experimental.pallas import tpu as pltpu
from jax.sharding import PartitionSpec as P

NGROUP = 12
TILE = 512
TILE_OWN = 8
SPANS = 64
WAFERS = 4
PLANE = 8
CORES = 2
ROWS = PLANE // CORES
DEPTH = SPANS // PLANE
DEV_DETS = 6
SENT = 2 * DEV_DETS + 1
WAFER_DETS = SPANS * DEV_DETS
SPAN_LEN = 256
NT = 64
HIT = 64
LANES = 128
CHUNK = 4
GROUPS = 4
FIRST_GROUPS = 3
GROUP_TIMES = SPAN_LEN // GROUPS

f32 = jnp.float32
bf16 = jnp.bfloat16
HIGHEST = lax.Precision.HIGHEST
VMEM = pl.BlockSpec(memory_space=pltpu.VMEM)
SMEM = pl.BlockSpec(memory_space=pltpu.SMEM)
ANY = pl.BlockSpec(memory_space=pl.ANY)


def call(kernel, out_shape, name, in_specs, scratch_shapes=(), vmem=16):
    return pl.pallas_call(
        kernel,
        out_shape=out_shape,
        in_specs=in_specs,
        out_specs=jax.tree.map(lambda unused: VMEM, out_shape),
        scratch_shapes=scratch_shapes,
        name=name,
        compiler_params=pltpu.CompilerParams(vmem_limit_bytes=vmem << 20),
        cost_estimate=pl.CostEstimate(flops=1 << 30, bytes_accessed=1 << 20, transcendentals=0),
    )


def split3(value):
    high = value.astype(bf16)
    rest = value - high.astype(f32)
    middle = rest.astype(bf16)
    low = (rest - middle.astype(f32)).astype(bf16)
    return high, middle, low


def exact_left_dot(left, right):
    return sum(jnp.dot(left, piece, preferred_element_type=f32) for piece in split3(right))


def pack_kernel(stream_ref, templates_ref, out_ref):
    templates = templates_ref[...]
    gram = lax.dot_general(
        templates, jnp.concatenate([templates, jnp.zeros_like(templates)], axis=0), (((1,), (1,)), ((), ())),
        precision=HIGHEST, preferred_element_type=f32,
    )
    for s in range(SPANS):
        for half in range(2):
            first = s * SPAN_LEN + half * LANES
            out_ref[pl.ds(s * SENT + half, DEV_DETS, stride=2), :] = stream_ref[:, first : first + LANES]
    out_ref[pl.ds(2 * DEV_DETS, SPANS, stride=SENT), :] = gram


def received_rows(received_ref):
    def rows(i, half):
        return jnp.concatenate(
            [received_ref[pl.ds(p * SENT + 2 * i + half, DEPTH, stride=PLANE * SENT), :] for p in range(PLANE)], axis=0
        )

    return jnp.concatenate(
        [jnp.concatenate([rows(i, 0), rows(i, 1)], axis=1) for i in range(DEV_DETS)], axis=0
    )


def lines(group_row):
    line = lax.broadcasted_iota(jnp.int32, (16, WAFER_DETS), 0)
    return jnp.where(line == group_row, 1.0, 0.0).astype(bf16)


def plane_total_kernel(received_ref, after_ref, out_ref):
    rows = DEPTH * CHUNK
    total = received_ref[0:rows, :]
    for k in range(1, PLANE):
        total = total + received_ref[rows * k : rows * (k + 1), :]
    gram_rows = received_ref[pl.ds(3, PLANE, stride=rows), :]
    for k in range(DEPTH):
        out_ref[rows * k : rows * (k + 1), :] = total
        out_ref[pl.ds(rows * k + 3, PLANE, stride=CHUNK), :] = gram_rows


def depth_total_kernel(received_ref, after_ref, out_ref):
    rows = DEPTH * CHUNK
    total = received_ref[0:rows, :]
    for k in range(1, DEPTH):
        total = total + received_ref[rows * k : rows * (k + 1), :]
    out_ref[...] = total


def factor_kernel(received_ref, templates_ref, after_ref, out_ref, solved_ref):
    gram = received_ref[pl.ds(3, SPANS, stride=CHUNK), :]
    lane = lax.broadcasted_iota(jnp.int32, (NT, LANES), 1)
    row = lax.broadcasted_iota(jnp.int32, (NT, LANES), 0)
    work = jnp.where(lane < NT, gram, jnp.where(lane - NT == row, 1.0, 0.0))
    blocks = [work[8 * b : 8 * b + 8, :] for b in range(NT // 8)]
    sublane = lax.broadcasted_iota(jnp.int32, (8, LANES), 0)

    def lane_spread(block, k):
        return jnp.broadcast_to(block[:, k : k + 1], (8, LANES))

    for b in range(NT // 8):
        first = 8 * b
        rows = [jnp.broadcast_to(blocks[b][i : i + 1, :], (8, LANES)) for i in range(8)]
        corner = {(i, j): lane_spread(rows[i], first + j) for i in range(8) for j in range(i, 8)}
        columns = [[lane_spread(block, first + j) for block in blocks[b:]] for j in range(8)]
        for i in range(8):
            inverse = 1.0 / corner[i, i]
            ratios = [column * inverse for column in columns[i]]
            ratios[0] = jnp.where(sublane > i, ratios[0], 0.0)
            blocks[b:] = [block - ratio * rows[i] for block, ratio in zip(blocks[b:], ratios)]
            for j in range(i + 1, 8):
                shift = corner[i, j] * inverse
                rows[j] = rows[j] - shift * rows[i]
                columns[j] = [later - earlier * shift for later, earlier in zip(columns[j], columns[i])]
                for k in range(j, 8):
                    corner[j, k] = corner[j, k] - shift * corner[i, k]
    work = jnp.concatenate(blocks, axis=0)
    pivots = jnp.sum(jnp.where(lane == row, work, 0.0), axis=1, keepdims=True)
    inverse = work * lax.rsqrt(pivots)
    swapped = pltpu.roll(inverse, NT, 1)
    out_ref[...] = jnp.where(lane < NT, swapped, 0.0)
    solved_ref[...] = jnp.dot(
        swapped[:, :NT], templates_ref[...], precision=HIGHEST, preferred_element_type=f32
    )


def prepare_kernel(
    own_ref, pointing_ref, weight_hbm, start_hbm, length_hbm, after_ref, coarse_ref, fine_ref, sample_weight_ref,
    weight_ref, start_ref, length_ref, semaphores
):
    copies = [
        pltpu.make_async_copy(source, target, semaphores.at[k])
        for k, (source, target) in enumerate(
            ((weight_hbm, weight_ref), (start_hbm, start_ref), (length_hbm, length_ref))
        )
    ]
    for copy in copies:
        copy.start()
    pointing = pointing_ref[...]
    coarse_ref[...] = (pointing >> 8).astype(f32).T
    fine = (pointing & 255).astype(f32)
    for g in range(GROUPS):
        fine_ref[g] = fine[:, g * GROUP_TIMES : (g + 1) * GROUP_TIMES]
    time = lax.broadcasted_iota(jnp.int32, (SPAN_LEN, WAFER_DETS), 0) + own_ref[0] * SPAN_LEN
    for copy in copies:
        copy.wait()
    start = start_ref[...].reshape(1, WAFER_DETS)
    stop = start + length_ref[...].reshape(1, WAFER_DETS)
    inside = (time >= start) & (time < stop)
    weight = jnp.broadcast_to(weight_ref[...].reshape(1, WAFER_DETS), (SPAN_LEN, WAFER_DETS))
    sample_weight_ref[...] = jnp.where(inside, 0.0, weight).astype(bf16).astype(f32)


def project_kernel(received_ref, group_ref, templates_ref, after_ref, out_ref):
    templates = templates_ref[...]
    twice = jnp.concatenate([templates, templates], axis=0)
    received = received_rows(received_ref)

    def project(rows):
        return lax.dot_general(
            rows, twice, (((1,), (1,)), ((), ())), precision=HIGHEST, preferred_element_type=f32
        )

    raw = project(received)
    onehot = lines(group_ref[...])
    means = project(exact_left_dot(onehot, received) * (NGROUP / WAFER_DETS))
    mixed = raw - sum(
        lax.dot_general(onehot, piece, (((0,), (0,)), ((), ())), preferred_element_type=f32) for piece in split3(means)
    )
    first_half = lax.broadcasted_iota(jnp.int32, (SPANS, LANES), 1) < NT
    for r in range(3):
        out_ref[pl.ds(r, SPANS, stride=CHUNK), :] = jnp.where(
            first_half, mixed[r * SPANS : (r + 1) * SPANS], mixed[(r + 3) * SPANS : (r + 4) * SPANS]
        )
    gram_row = jnp.sum(received_ref[pl.ds(2 * DEV_DETS, SPANS, stride=SENT), :], axis=0, keepdims=True)
    out_ref[pl.ds(3, SPANS, stride=CHUNK), :] = jnp.broadcast_to(gram_row, (SPANS, LANES))


def clean_kernel(received_ref, column_ref, row_ref, after_ref, out_ref):
    row = lax.broadcasted_iota(jnp.int32, (WAFER_DETS, WAFER_DETS), 0)
    column = lax.broadcasted_iota(jnp.int32, (WAFER_DETS, WAFER_DETS), 1)
    det = ((row % DEPTH) * PLANE + (row % SPANS) // DEPTH) * DEV_DETS + row // SPANS
    keep = jnp.where(det == column, 1.0, 0.0)
    mixer = (keep - jnp.where(column_ref[...] == row_ref[...], NGROUP / WAFER_DETS, 0.0)).astype(bf16)
    out_ref[...] = sum(
        lax.dot_general(piece, mixer, (((0,), (0,)), ((), ())), preferred_element_type=f32)
        for piece in split3(received_rows(received_ref))
    )


def accumulate(values_ref, coarse_ref, fine_ref, totals_ref, first, last, unroll=1):
    labels = lax.broadcasted_iota(jnp.int32, (LANES, WAFER_DETS), 0).astype(f32).astype(bf16)
    lane = lax.broadcasted_iota(jnp.int32, (WAFER_DETS, LANES), 1)
    low_lane, high_lane = lane.astype(f32).astype(bf16), (lane + LANES).astype(f32).astype(bf16)
    one, zero = jnp.ones((WAFER_DETS, LANES), bf16), jnp.zeros((WAFER_DETS, LANES), bf16)
    blank = jnp.zeros((16, WAFER_DETS), bf16)

    def spread(rows, i):
        return jnp.broadcast_to(rows[i : i + 1], (16, WAFER_DETS)).astype(bf16)

    def step(g, carry):
        fine = fine_ref[g]
        left, right = [], []
        for block in range(GROUP_TIMES // 8):
            times = pl.ds(pl.multiple_of(g * GROUP_TIMES + 8 * block, 8), 8)
            coarse_rows, value_rows = coarse_ref[times, :], values_ref[times, :]
            for i in range(8):
                coarse, value = spread(coarse_rows, i), spread(value_rows, i)
                left.append(
                    jnp.concatenate(
                        [jnp.where(labels[16 * m : 16 * m + 16] == coarse, value, blank) for m in range(8)], axis=0
                    )
                )
                t = 8 * block + i
                point = jnp.broadcast_to(fine[:, t : t + 1], (WAFER_DETS, LANES)).astype(bf16)
                right.append(
                    jnp.concatenate(
                        [jnp.where(low_lane == point, one, zero), jnp.where(high_lane == point, one, zero)], axis=1
                    )
                )
        totals_ref[...] += jnp.dot(
            jnp.concatenate(left, axis=1), jnp.concatenate(right, axis=0), preferred_element_type=f32
        )
        return carry

    lax.fori_loop(first, last, step, 0, unroll=unroll)


def weight_first_kernel(sample_weight_ref, coarse_ref, fine_ref, out_ref):
    out_ref[...] = jnp.zeros_like(out_ref)
    accumulate(sample_weight_ref, coarse_ref, fine_ref, out_ref, 0, FIRST_GROUPS)


def weight_rest_kernel(sample_weight_ref, coarse_ref, fine_ref, totals_ref, after_ref, out_ref):
    out_ref[...] = totals_ref[...]
    accumulate(sample_weight_ref, coarse_ref, fine_ref, out_ref, FIRST_GROUPS, GROUPS)


def bin_kernel(
    place_ref, gathered_ref, inverse_ref, solved_ref, cleaned_ref, sample_weight_ref, coarse_ref, fine_ref,
    weight_totals_ref, out_ref, values, totals, halves, ordered
):
    for p in range(PLANE):
        block = place_ref[p]
        for r in range(3):
            rows = gathered_ref.at[block][pl.ds(r, DEPTH, stride=CHUNK), :]
            for half in range(2):
                target = pl.ds(p * DEV_DETS + half * 3 + r, DEPTH, stride=PLANE * DEV_DETS)
                ordered[target, :] = pltpu.roll(rows, NT, 1) if half else rows
    middle = lax.dot_general(
        ordered[...], inverse_ref[...], (((1,), (1,)), ((), ())), precision=HIGHEST, preferred_element_type=f32
    )
    fitted = lax.dot_general(
        solved_ref[...], middle, (((0,), (1,)), ((), ())), precision=HIGHEST, preferred_element_type=f32
    )
    values[...] = sample_weight_ref[...] * (cleaned_ref[...] - fitted)
    totals[...] = jnp.zeros_like(totals)
    accumulate(values, coarse_ref, fine_ref, totals, 0, GROUPS, unroll=2)
    for kind, source_ref in enumerate((totals, weight_totals_ref)):
        for column in range(2):
            halves[...] = source_ref[:, column * LANES : (column + 1) * LANES]
            for half in range(2):
                out_ref[half * 2 + column, kind * HIT : (kind + 1) * HIT, :] = halves[pl.ds(half, HIT, stride=2), :]


def coeffs_kernel(gathered_ref, inverse_ref, after_ref, out_ref):
    inverse = inverse_ref[:, :NT]
    gathered = gathered_ref[...]
    for half in range(2):
        middle = lax.dot_general(
            gathered[:, half * NT : half * NT + NT], inverse, (((1,), (1,)), ((), ())),
            precision=HIGHEST, preferred_element_type=f32,
        )
        coeffs = jnp.dot(middle, inverse, precision=HIGHEST, preferred_element_type=f32)
        out_ref[half * 3 : half * 3 + 3, :] = coeffs[0:3, :]


def route_kernel(first_ref, second_ref, third_ref, fourth_ref, slot_ref, out_ref):
    total = first_ref[...] + second_ref[...] + third_ref[...] + fourth_ref[...]
    row = lax.broadcasted_iota(jnp.int32, (SPANS * CHUNK, 2 * HIT), 0)
    selector = jnp.where(row == slot_ref[...], 1.0, 0.0).astype(bf16)
    out_ref[...] = exact_left_dot(selector, total)


def merge_kernel(received_ref, tile_ref, rhs_ref, weight_ref):
    rows = SPANS * CHUNK
    wanted = lax.broadcasted_iota(jnp.int32, (16, rows), 0)
    column = lax.broadcasted_iota(jnp.int32, (16, rows), 1)
    chosen = (tile_ref[...] == wanted % 8) & ((column % CHUNK) // 2 == wanted // 8)
    selector = jnp.where(chosen, 1.0, 0.0).astype(bf16)
    merged = exact_left_dot(selector, received_ref[...])
    rhs_ref[...] = merged[0:8, :]
    weight_ref[...] = merged[8:16, :]


def shape(*dims, dtype=f32):
    return jax.ShapeDtypeStruct(dims, dtype)


def exchange(values, axes, *dims):
    return lax.all_to_all(values.reshape(dims), axes, split_axis=0, concat_axis=0, tiled=True)


def body(timestream, templates, bias_group, det_weight, cut_start, cut_len, pointing, hit_tiles):
    plane = ("row", "core")
    span = ("depth", *plane)
    own = lax.axis_index(span)
    outgoing = call(pack_kernel, shape(SPANS * SENT, LANES), "pack", [VMEM, VMEM], vmem=60)(timestream, templates)
    received = exchange(outgoing, span, SPANS, 1, SENT * LANES).reshape(SPANS * SENT, LANES)

    groups = bias_group.reshape(DEPTH, PLANE, DEV_DETS).transpose(2, 1, 0).reshape(WAFER_DETS)
    coarse, fine, sample_weight = call(
        prepare_kernel,
        (shape(SPAN_LEN, WAFER_DETS), shape(GROUPS, WAFER_DETS, GROUP_TIMES), shape(SPAN_LEN, WAFER_DETS)),
        "prepare", [SMEM, VMEM] + [ANY] * 4,
        [
            pltpu.VMEM((WAFER_DETS,), f32), pltpu.VMEM((WAFER_DETS,), jnp.int32), pltpu.VMEM((WAFER_DETS,), jnp.int32),
            pltpu.SemaphoreType.DMA((3,)),
        ],
    )(own.reshape(1), pointing, det_weight, cut_start, cut_len, outgoing)
    weight_totals = call(weight_first_kernel, shape(LANES, 2 * LANES), "weight_first", [VMEM] * 3, vmem=24)(
        sample_weight, coarse, fine
    )
    order = jnp.arange(HIT, dtype=jnp.int32)
    own_owner = lax.dynamic_index_in_dim(hit_tiles, own, 0, keepdims=False) // TILE_OWN
    earlier = (own_owner[None, :] == own_owner[:, None]) & (order[None, :] < order[:, None])
    base = own_owner * CHUNK + jnp.sum(earlier.astype(jnp.int32), axis=1)
    slot = jnp.concatenate([base, base + 2])[None, :]
    mine = hit_tiles // TILE_OWN == own
    position = jnp.broadcast_to(order[None, :], (SPANS, HIT))
    first = jnp.min(jnp.where(mine, position, HIT), axis=1, keepdims=True)
    last = jnp.max(jnp.where(mine, position, -1), axis=1, keepdims=True)
    within = hit_tiles % TILE_OWN + 1
    first_tile = jnp.sum(jnp.where(position == first, within, 0), axis=1) - 1
    last_tile = jnp.sum(jnp.where(position == last, within, 0), axis=1) - 1
    slot_tile = jnp.stack([first_tile, last_tile, first_tile, last_tile], axis=1).reshape(1, SPANS * CHUNK)

    partial = call(project_kernel, shape(SPANS * CHUNK, LANES), "project", [VMEM] * 3 + [ANY])(
        received, groups[None, :], templates, weight_totals
    )
    reduced = exchange(partial, plane, PLANE, DEPTH * CHUNK, LANES).reshape(SPANS * CHUNK, LANES)
    weight_totals = call(weight_rest_kernel, shape(LANES, 2 * LANES), "weight_rest", [VMEM] * 4 + [ANY], vmem=24)(
        sample_weight, coarse, fine, weight_totals, partial
    )
    reduced = call(plane_total_kernel, shape(SPANS * CHUNK, LANES), "plane_total", [VMEM, ANY])(reduced, weight_totals)
    cleaned = call(clean_kernel, shape(SPAN_LEN, WAFER_DETS), "clean", [VMEM] * 3 + [ANY])(
        received, groups[:, None], bias_group[None, :], reduced
    )
    reduced = exchange(reduced, "depth", DEPTH, PLANE * CHUNK, LANES).reshape(SPANS * CHUNK, LANES)
    totals = call(depth_total_kernel, shape(DEPTH * CHUNK, LANES), "depth_total", [VMEM, ANY])(reduced, cleaned)
    partner = lax.ppermute(totals, "core", [(0, 1), (1, 0)])
    pair = jnp.concatenate([totals, partner], axis=0)
    pairs = [pair] + [
        lax.ppermute(pair, "row", [(x, (x + k) % ROWS) for x in range(ROWS)]) for k in (1, 2, 3)
    ]
    own_row, own_core = lax.axis_index("row"), lax.axis_index("core")
    gathered = jnp.concatenate(pairs, axis=0).reshape(PLANE, DEPTH * CHUNK, LANES)
    block = jnp.arange(PLANE, dtype=jnp.int32)
    places = (own_row + ROWS - block // CORES) % ROWS * CORES + (own_core + block) % CORES
    inverse, solved = call(factor_kernel, (shape(NT, LANES), shape(NT, SPAN_LEN)), "factor", [VMEM] * 2 + [ANY])(
        reduced, templates, pair
    )
    tiles = call(
        bin_kernel, shape(WAFERS, 2 * HIT, LANES), "bin", [SMEM] + [VMEM] * 8,
        [
            pltpu.VMEM((SPAN_LEN, WAFER_DETS), f32), pltpu.VMEM((LANES, 2 * LANES), f32),
            pltpu.VMEM((LANES, LANES), f32), pltpu.VMEM((WAFER_DETS, LANES), f32),
        ],
        vmem=24,
    )(places, gathered, inverse, solved, cleaned, sample_weight, coarse, fine, weight_totals)
    own_wafer = lax.axis_index("wafer")
    tiles = [
        lax.ppermute(
            lax.dynamic_index_in_dim(tiles, (own_wafer + k) % WAFERS, 0, keepdims=False), "wafer",
            [(w, (w + k) % WAFERS) for w in range(WAFERS)],
        ) if k else lax.dynamic_index_in_dim(tiles, own_wafer, 0, keepdims=False)
        for k in range(WAFERS)
    ]
    routed = call(route_kernel, shape(SPANS * CHUNK, LANES), "route", [VMEM] * 5)(*tiles, slot)
    sent = routed
    routed = exchange(routed, span, SPANS, CHUNK, LANES).reshape(SPANS * CHUNK, LANES)
    own_rows = lax.dynamic_slice_in_dim(totals, lax.axis_index("depth") * CHUNK, CHUNK)
    own_rows = jnp.concatenate([own_rows, own_rows], axis=0)
    fit_coeffs = call(coeffs_kernel, shape(DEV_DETS, NT), "coeffs", [VMEM] * 2 + [ANY])(own_rows, inverse, sent)
    rhs_map, weight_map = call(merge_kernel, (shape(8, LANES), shape(8, LANES)), "merge", [VMEM, VMEM])(
        routed, slot_tile
    )
    return (fit_coeffs, rhs_map, weight_map)


def solution(mesh):
    mesh = jax.sharding.Mesh(mesh.devices.reshape(WAFERS, DEPTH, ROWS, CORES), ("wafer", "depth", "row", "core"))
    span = ("depth", "row", "core")
    in_specs = (
        P(("wafer", *span), None),
        P(None, span),
        P("wafer"),
        P("wafer"),
        P("wafer"),
        P("wafer"),
        P("wafer", span),
        P(),
    )
    out_specs = (P(("wafer", *span), None), P(span, "wafer"), P(span, "wafer"))
    return jax.shard_map(body, mesh=mesh, in_specs=in_specs, out_specs=out_specs, check_vma=False)
```
